32 devices in a mesh: mem: 4 (over x, core), lat: 8 (over z, y).
Axes of the slice: x: 2, y: 2, z: 4, core: 2. Of those that a mesh axis runs over, the one named last changes fastest.
Arguments:
- ensemble: float32 [256, 16, 512], P('mem', 'lat'), may hold values from -6 to 6
- diffusivity: float32 [16, 512], P('lat'), may hold values from 0.02 to 0.2
- north_wind: float32 [16, 512], P('lat'), may hold values from -0.25 to 0.25
- observed_blocks: int32 [8, 4, 4], P('lat'), may hold values from 0 to 7
- eastern_average_flags: int32 [8, 4, 512], P('lat'), may hold values 0 or 1
- observed_values: float32 [8, 4, 512], P('lat', 'mem'), may hold values from -6 to 6
- observed_error: float32 [8, 4, 512], P('lat', 'mem'), may hold values from 0.5 to 4
Outputs:
- analysis: float32 [256, 16, 512], P('mem', 'lat')
The draws below stay inside these ranges and needn't reach their ends.
Inputs may be any that keep to these rules, and one draw needn't show every extreme that they name: `observed_blocks`: block i covers a band's flattened cells i * 128 to (i + 1) * 128 - 1; blocks may repeat.
All inputs are finite; a program needn't handle non-finite values. No bound on the sum of `eastern_average_flags` on one device may be relied on, other than what follows from the above.
Results may differ from the reference program's by a relative error of at most 0.0003.
Values sent between devices are 32-bit elements; how exact they have to be, the bound alone decides.
No kernel may reach another device: no remote copies, remote signals or barrier semaphores. Data moves between devices by JAX's collectives and lax.ppermute only.
A program may use at most 64 MiB of HBM per device.

```python
import math
import jax
import jax.numpy as jnp
from jax import lax

ACELLS = 256
LON = 512
OBS = 512
BLOCK = 128
NEWTON = 4
MEMBERS = 256
PARALLEL_COUNT = 2
LAT = 16
BANDS = 8
PATCH_BAND = 4
NBLK = 4
BAND_BLOCKS = 8
N_MEM = 4
N_LAT = 8


def plant(array, own_key, least, high):
    dims = array.shape
    index_at = [jax.random.randint(jax.random.fold_in(own_key, axis), (), 0, dims[axis]) for axis in range(len(dims))]
    array = array.at[tuple(index_at)].set(least)
    longest = dims.index(max(dims))
    index_at[longest] = (index_at[longest] + 1) % dims[longest]
    return array.at[tuple(index_at)].set(high)


def steps_of(own_key, shape, cuts, least, top_value):
    def one(position, parts):
        heights = jax.random.uniform(jax.random.fold_in(jax.random.fold_in(own_key, 6), position), (parts,), jnp.float32, least / len(cuts), top_value / len(cuts))
        return jnp.repeat(jnp.exp(heights), shape[position] // parts).reshape((-1,) + (1,) * (len(shape) - position - 1))

    level = one(*cuts[0])
    for cut in cuts[1:]:
        level = level * one(*cut)
    return level


def normal_values(own_key, dims, deviation, limit, cuts=(), kind=jnp.bfloat16):
    entries = jax.random.normal(own_key, dims, jnp.float32) * deviation
    if len(cuts) > 0:
        entries = steps_of(own_key, dims, cuts, -0.22, 0.18) * entries
    return jnp.clip(entries, min=-limit, max=limit).astype(kind)


def setup_inputs(seed: int = 0) -> dict:
    key_of = jax.random.split(jax.random.key(seed), 8)
    return {
        "ensemble": normal_values(key_of[0], (MEMBERS, LAT, LON), 1.0, 6.0, ((0, 4), (1, 8)), jnp.float32),
        "diffusivity": jnp.clip(jnp.exp(math.log(0.2) - 2.3025851 * jax.random.uniform(key_of[1], (LAT, LON), jnp.float32) ** steps_of(key_of[1], (LAT, LON), ((0, 8),), -0.2, 0.2)), 0.02, 0.2),
        "north_wind": jnp.clip(jax.random.uniform(key_of[2], (LAT, LON), jnp.float32, -0.25, 0.25) * steps_of(key_of[2], (LAT, LON), ((0, 8),), -0.4, 0.0), -0.25, 0.25),
        "observed_blocks": plant(jax.random.randint(key_of[3], (BANDS, PATCH_BAND, NBLK), 0, BAND_BLOCKS), jax.random.fold_in(key_of[3], 1), 0, BAND_BLOCKS - 1).astype(jnp.int32),
        "eastern_average_flags": plant((jax.random.randint(key_of[4], (BANDS, PATCH_BAND, OBS), 0, 2) < 1).astype(jnp.int32), jax.random.fold_in(key_of[4], 1), 0, 1),
        "observed_values": normal_values(key_of[5], (BANDS, PATCH_BAND, OBS), 1.0, 6.0, ((0, 8), (1, 4)), jnp.float32),
        "observed_error": jnp.clip(jnp.exp(math.log(4.0) - 2.0794415 * jax.random.uniform(key_of[6], (BANDS, PATCH_BAND, OBS), jnp.float32) ** steps_of(key_of[6], (BANDS, PATCH_BAND, OBS), ((0, 8), (1, 4)), -0.2, 0.2)), 0.5, 4.0),
    }


ADVECTION = 0.1
HIGHEST = lax.Precision.HIGHEST


def advance(padded, diffusivity, north_wind):
    centre = padded[:, 1:-1, :]
    northern = padded[:, :-2, :]
    equatorward_side = padded[:, 2:, :]
    eastern = jnp.roll(centre, -1, axis=2)
    western_neighbour = jnp.roll(centre, 1, axis=2)
    return centre - ADVECTION * centre * (eastern - western_neighbour) - north_wind * (equatorward_side - northern) + diffusivity * (eastern + western_neighbour + northern + equatorward_side - 4.0 * centre)


def contract_first(left, right):
    return lax.dot_general(left, right, (((0,), (0,)), ((), ())), precision=HIGHEST, preferred_element_type=jnp.float32)


def patch_gain(cell_values, seen_values, values, errors):
    sample_states = cell_values.shape[0]
    cell_offset = cell_values - jnp.mean(cell_values, axis=0)
    seen_mean = jnp.mean(seen_values, axis=0)
    seen_offset = seen_values - seen_mean
    covariance = contract_first(seen_offset, seen_offset) / (sample_states - 1.0) + jnp.diag(errors)
    row_scale = jnp.sum(jnp.abs(covariance), axis=1)
    inverse = jnp.diag(1.0 / row_scale)
    for sweep in range(NEWTON):
        product = jnp.dot(covariance, inverse, precision=HIGHEST, preferred_element_type=jnp.float32)
        inverse = 2.0 * inverse - jnp.dot(inverse, product, precision=HIGHEST, preferred_element_type=jnp.float32)
    cross_cov = contract_first(cell_offset, seen_offset) / (sample_states - 1.0)
    gain = jnp.dot(cross_cov, inverse, precision=HIGHEST, preferred_element_type=jnp.float32)
    innovation = values - seen_mean
    return gain, innovation, seen_mean


def reference(ensemble, diffusivity, north_wind, observed_blocks, eastern_average_flags, observed_values, observed_error):
    sample_states, latitudes, meridian_total = ensemble.shape
    sample_partitions = ensemble.reshape(N_MEM, sample_states // N_MEM, latitudes, meridian_total)

    def background_state(variable_layers):
        for sweep in range(2):
            padded = jnp.pad(variable_layers, ((0, 0), (1, 1), (0, 0)))
            variable_layers = advance(padded, diffusivity, north_wind)
        return variable_layers

    variable_layers = lax.map(background_state, sample_partitions).reshape(sample_states, N_LAT, PARALLEL_COUNT * meridian_total)

    def patch(patch_index):
        band_index = patch_index // N_MEM
        segment_number = patch_index % N_MEM
        band_flat = lax.dynamic_index_in_dim(variable_layers, band_index, axis=1, keepdims=False)
        band_grid = band_flat.reshape(sample_states, PARALLEL_COUNT, meridian_total)
        block_tiles = band_flat.reshape(sample_states, -1, BLOCK)
        east_tiles = jnp.roll(band_grid, -1, axis=2).reshape(sample_states, -1, BLOCK)
        chosen = observed_blocks[band_index, segment_number].astype(jnp.int32)
        direct = jnp.take(block_tiles, chosen, axis=1).reshape(sample_states, OBS)
        shifted = jnp.take(east_tiles, chosen, axis=1).reshape(sample_states, OBS)
        lag_flags = eastern_average_flags[band_index, segment_number]
        seen_values = jnp.where(lag_flags[None, :] == 1, 0.5 * (direct + shifted), direct)
        cell_values = lax.dynamic_slice_in_dim(band_flat, (segment_number * ACELLS).astype(jnp.int32), ACELLS, axis=1)
        gain, innovation, seen_mean = patch_gain(cell_values, seen_values, observed_values[band_index, segment_number], observed_error[band_index, segment_number])
        weights = innovation[None, :] - 0.5 * (seen_values - seen_mean[None, :])
        update = lax.dot_general(weights, gain, (((1,), (1,)), ((), ())), precision=HIGHEST, preferred_element_type=jnp.float32)
        return cell_values + update

    result = lax.map(patch, jnp.arange(N_LAT * N_MEM, dtype=jnp.int32))
    result = result.reshape(N_LAT, N_MEM, sample_states, ACELLS).transpose(2, 0, 1, 3)
    return result.reshape(sample_states, latitudes, meridian_total)
```

```python
import functools

import jax
import jax.numpy as jnp
from jax import lax
from jax.experimental import pallas as pl
from jax.experimental.pallas import tpu as pltpu
from jax.sharding import PartitionSpec as P

NEWTON = 4
ADVECTION = 0.1
F32 = jnp.float32
BF16 = jnp.bfloat16
VMEM = pl.BlockSpec(memory_space=pltpu.VMEM)
SMEM = pl.BlockSpec(memory_space=pltpu.SMEM)


def xor_pairs(count, bit):
    return [(i, i ^ bit) for i in range(count)]


def step(rows, diffusivity, north_wind):
    out = []
    for r in range(1, len(rows) - 1):
        north, centre, south = rows[r - 1], rows[r], rows[r + 1]
        last = centre.shape[1] - 1
        eastern = pltpu.roll(centre, last, 1)
        western = pltpu.roll(centre, 1, 1)
        out.append(
            centre
            - ADVECTION * centre * (eastern - western)
            - north_wind[r - 1] * (south - north)
            + diffusivity[r - 1] * (eastern + western + north + south - 4.0 * centre)
        )
    return out


def forecast_kernel(first, count, lead, own, dif, wind, near, far, coef_near, coef_far, out):
    even = lax.rem(lax.axis_index("lat"), 2) == 0
    rows, longitudes = own.shape[1], own.shape[2]
    edge = near.shape[1]

    def pick(a, b):
        return jnp.where(even, a, b)

    def members(ref, r):
        return ref[lead : lead + count, r, :]

    low = [pick(members(far, r), members(near, r)) for r in (edge - 2, edge - 1)]
    high = [pick(members(near, r), members(far, r)) for r in (0, 1)]
    here = [own[first : first + count, r, :] for r in range(rows)]

    def coefficient(which, ref):
        before = pick(coef_far[which : which + 1, edge - 1, :], coef_near[which : which + 1, edge - 1, :])
        after = pick(coef_near[which : which + 1, 0, :], coef_far[which : which + 1, 0, :])
        return [before] + [ref[r : r + 1, :] for r in range(rows)] + [after]

    d, w = coefficient(0, dif), coefficient(1, wind)
    once = step(low + here + high, d, w)
    twice = step(once, d[1:-1], w[1:-1])
    for r in range(rows):
        out[:, r * longitudes : (r + 1) * longitudes] = twice[r]


def split(x):
    high = x.astype(BF16)
    return high, (x - high.astype(F32)).astype(BF16)


def dot3(a, b, dims=(((1,), (0,)), ((), ()))):
    mul = functools.partial(lax.dot_general, dimension_numbers=dims, preferred_element_type=F32)
    return mul(a[0], b[0]) + (mul(a[0], b[1]) + mul(a[1], b[0]))


def gain_kernel(groups, pieces, tops, longitudes, blocks, flags, values, errors, *refs):
    parts = refs[: groups * pieces]
    outs = refs[groups * pieces : -2]
    seen, cells = refs[-2:]
    patch = lax.axis_index("mem")
    total, observations = seen.shape
    own_cells = cells.shape[1]
    block_count = blocks.shape[1]
    width = observations // block_count
    row_blocks = longitudes // width
    flag = flags[pl.ds(patch, 1), :]
    lane = lax.broadcasted_iota(jnp.int32, (1, width), 1)
    for i in range(block_count):
        c = blocks[patch, i]
        row = lax.div(c, row_blocks)
        n = row * row_blocks + lax.rem(c - row * row_blocks + 1, row_blocks)
        averaged = flag[:, i * width : (i + 1) * width] == 1
        at = 0
        for part in parts:
            size = part.shape[0]
            direct = part[:, pl.ds(pl.multiple_of(c * width, width), width)]
            beyond = part[:, pl.ds(pl.multiple_of(n * width, width), width)]
            east = jnp.where(
                lane == width - 1, pltpu.roll(beyond, width - 1, 1), pltpu.roll(direct, width - 1, 1)
            )
            seen[at : at + size, i * width : (i + 1) * width] = jnp.where(
                averaged, 0.5 * (direct + east), direct
            )
            at += size
    at = 0
    for part in parts:
        size = part.shape[0]
        cells[at : at + size, :] = part[:, pl.ds(pl.multiple_of(patch * own_cells, own_cells), own_cells)]
        at += size
    scale = 1.0 / (total - 1.0)
    raw = seen[...]
    seen_mean = jnp.sum(raw, axis=0, keepdims=True) * (1.0 / total)
    offset = raw - seen_mean
    off = split(offset)
    turned = split(offset.T)
    covariance = dot3(turned, off) * scale
    down = lax.broadcasted_iota(jnp.int32, covariance.shape, 0)
    across = lax.broadcasted_iota(jnp.int32, covariance.shape, 1)
    covariance = covariance + jnp.where(down == across, errors[...], 0.0)
    inverse_scale = 1.0 / jnp.sum(jnp.abs(covariance), axis=0, keepdims=True)
    start = ((values[...] - seen_mean) - 0.5 * offset) * inverse_scale
    b1 = covariance * inverse_scale
    s1 = split(b1)
    b2 = 2.0 * b1 - dot3(s1, s1)
    s2 = split(b2)
    b4 = 2.0 * b2 - dot3(s2, s2)
    s4 = split(b4)
    q = start
    for _ in range(3):
        q = start + (q - dot3(split(q), s4))
    q = 2.0 * q - dot3(split(q), s2)
    q = 2.0 * q - dot3(split(q), s1)
    mix = dot3(split(q), off, (((1,), (1,)), ((), ()))) * scale
    state = cells[...]
    shift = state - jnp.sum(state, axis=0, keepdims=True) * (1.0 / total)
    analysed = state + dot3(split(mix), split(shift))
    size = total // groups
    for out, wanted in zip(outs, tops):
        for at, j in enumerate(wanted):
            out[at * size : (at + 1) * size, :] = analysed[j * size : (j + 1) * size, :]


def place_kernel(masks, where, longitudes, *refs):
    sources, out = refs[:-1], refs[-1]
    here = lax.axis_index("mem")
    local = out.shape[0]
    width = sources[0].shape[1]
    found = [sources[where[m][0]][where[m][1] * local : (where[m][1] + 1) * local, :] for m in masks]
    for patch in range(len(masks)):
        value = found[0]
        for m, candidate in zip(masks[1:], found[1:]):
            value = jnp.where((here ^ m) == patch, candidate, value)
        row, column = divmod(patch * width, longitudes)
        out[:, row, column : column + width] = value


def body(
    ensemble,
    diffusivity,
    north_wind,
    observed_blocks,
    eastern_average_flags,
    observed_values,
    observed_error,
):
    local, rows, longitudes = ensemble.shape
    lats, mems = lax.axis_size("lat"), lax.axis_size("mem")
    observations = observed_values.shape[-1]
    cell_count = rows * longitudes
    own_cells = cell_count // mems
    total = local * mems
    near_pairs = xor_pairs(lats, 1)
    far_pairs = [(i, i + 2) for i in range(0, lats - 2, 2)] + [(i, i - 2) for i in range(3, lats, 2)]

    def edges(block):
        if block.shape[1] == 2:
            return block
        return jnp.concatenate([block[:, :2], block[:, -2:]], axis=1)

    pieces = 2
    count = local // pieces
    bits = [1 << k for k in reversed(range(mems.bit_length() - 1))]
    coefficients = edges(jnp.stack([diffusivity, north_wind]))
    near, far = [], []
    for k in range(pieces):
        own = edges(ensemble[k * count : (k + 1) * count])
        if k == 0:
            own = jnp.concatenate([coefficients, own], axis=0)
        near.append(lax.ppermute(own, "lat", near_pairs))
    for k in range(pieces):
        far.append(lax.ppermute(near[k], "lat", far_pairs))
    parts = [[] for _ in range(pieces)]
    for k in range(pieces):
        band = pl.pallas_call(
            functools.partial(forecast_kernel, k * count, count, 2 if k == 0 else 0),
            out_shape=jax.ShapeDtypeStruct((count, cell_count), F32),
            in_specs=[VMEM] * 7,
            out_specs=VMEM,
            cost_estimate=pl.CostEstimate(flops=2000000, bytes_accessed=2000000, transcendentals=0),
            name="forecast",
        )(ensemble, diffusivity, north_wind, near[k], far[k], near[0], far[0])
        held = [band]
        for bit in bits:
            held = held + [lax.ppermute(a, "mem", xor_pairs(mems, bit)) for a in held]
        parts[k] = held
    masks = [0]
    for bit in bits:
        masks = masks + [m ^ bit for m in masks]

    tops = [[j for j, m in enumerate(masks) if (m & bit) and m < 2 * bit] for bit in bits]
    tops.append([0])
    flat = [parts[k][j] for j in range(mems) for k in range(pieces)]
    shapes = [jax.ShapeDtypeStruct((len(t) * local, own_cells), F32) for t in tops]
    outs = pl.pallas_call(
        functools.partial(gain_kernel, mems, pieces, tops, longitudes),
        out_shape=shapes,
        in_specs=[SMEM] + [VMEM] * (3 + len(flat)),
        out_specs=[VMEM] * len(shapes),
        scratch_shapes=[pltpu.VMEM((total, observations), F32), pltpu.VMEM((total, own_cells), F32)],
        cost_estimate=pl.CostEstimate(flops=5000000000, bytes_accessed=4000000, transcendentals=0),
        name="gain",
    )(observed_blocks[0], eastern_average_flags[0], observed_values[0], observed_error[0], *flat)
    carried = [(outs[-1], [(0, 0)])]
    for bit, sent, top in zip(bits, outs, tops):
        moving = [(a, g) for a, g in carried if any(left & bit for left, _ in g)]
        moving.append((sent, [(masks[j], 0) for j in top]))
        stay = [(a, [(left if not left & bit else -1, pm) for left, pm in g]) for a, g in carried]
        came = [
            (
                lax.ppermute(a, "mem", xor_pairs(mems, bit)),
                [(left ^ bit if left > 0 and left & bit else -1, pm ^ bit) for left, pm in g],
            )
            for a, g in moving
        ]
        carried = stay + came
    where = {}
    for index, (_, g) in enumerate(carried):
        for at, (left, pm) in enumerate(g):
            if left == 0:
                where[pm] = (index, at)
    return pl.pallas_call(
        functools.partial(place_kernel, masks, where, longitudes),
        out_shape=jax.ShapeDtypeStruct((local, rows, longitudes), F32),
        in_specs=[VMEM] * len(carried),
        out_specs=VMEM,
        cost_estimate=pl.CostEstimate(flops=100000, bytes_accessed=600000, transcendentals=0),
        name="place",
    )(*[a for a, _ in carried])


def solution(mesh):
    return jax.shard_map(
        body,
        mesh=mesh,
        in_specs=(
            P("mem", "lat", None),
            P("lat", None),
            P("lat", None),
            P("lat", None, None),
            P("lat", None, None),
            P("lat", "mem", None),
            P("lat", "mem", None),
        ),
        out_specs=P("mem", "lat", None),
        check_vma=False,
    )
```

```python
import functools

import jax
import jax.numpy as jnp
from jax import lax
from jax.experimental import pallas as pl
from jax.experimental.pallas import tpu as pltpu
from jax.sharding import PartitionSpec as P

NEWTON = 4
ADVECTION = 0.1
F32 = jnp.float32
BF16 = jnp.bfloat16
VMEM = pl.BlockSpec(memory_space=pltpu.VMEM)
SMEM = pl.BlockSpec(memory_space=pltpu.SMEM)


def xor_pairs(count, bit):
    return [(i, i ^ bit) for i in range(count)]


def step(rows, diffusivity, north_wind):
    out = []
    for r in range(1, len(rows) - 1):
        north, centre, south = rows[r - 1], rows[r], rows[r + 1]
        last = centre.shape[1] - 1
        eastern = pltpu.roll(centre, last, 1)
        western = pltpu.roll(centre, 1, 1)
        out.append(
            centre
            - ADVECTION * centre * (eastern - western)
            - north_wind[r - 1] * (south - north)
            + diffusivity[r - 1] * (eastern + western + north + south - 4.0 * centre)
        )
    return out


def forecast_kernel(first, count, lead, own, dif, wind, near, far, coef_near, coef_far, out):
    even = lax.rem(lax.axis_index("lat"), 2) == 0
    rows, longitudes = own.shape[1], own.shape[2]
    edge = near.shape[1]

    def pick(a, b):
        return jnp.where(even, a, b)

    def members(ref, r):
        return ref[lead : lead + count, r, :]

    low = [pick(members(far, r), members(near, r)) for r in (edge - 2, edge - 1)]
    high = [pick(members(near, r), members(far, r)) for r in (0, 1)]
    here = [own[first : first + count, r, :] for r in range(rows)]

    def coefficient(which, ref):
        before = pick(coef_far[which : which + 1, edge - 1, :], coef_near[which : which + 1, edge - 1, :])
        after = pick(coef_near[which : which + 1, 0, :], coef_far[which : which + 1, 0, :])
        return [before] + [ref[r : r + 1, :] for r in range(rows)] + [after]

    d, w = coefficient(0, dif), coefficient(1, wind)
    once = step(low + here + high, d, w)
    twice = step(once, d[1:-1], w[1:-1])
    for r in range(rows):
        out[:, r * longitudes : (r + 1) * longitudes] = twice[r]


def split(x):
    high = x.astype(BF16)
    return high, (x - high.astype(F32)).astype(BF16)


def dot3(a, b, dims=(((1,), (0,)), ((), ()))):
    mul = functools.partial(lax.dot_general, dimension_numbers=dims, preferred_element_type=F32)
    return mul(a[0], b[0]) + (mul(a[0], b[1]) + mul(a[1], b[0]))


def gain_kernel(groups, pieces, tops, longitudes, blocks, flags, values, errors, *refs):
    parts = refs[: groups * pieces]
    outs = refs[groups * pieces : -2]
    seen, cells = refs[-2:]
    patch = lax.axis_index("mem")
    total, observations = seen.shape
    own_cells = cells.shape[1]
    block_count = blocks.shape[1]
    width = observations // block_count
    row_blocks = longitudes // width
    flag = flags[pl.ds(patch, 1), :]
    lane = lax.broadcasted_iota(jnp.int32, (1, width), 1)
    for i in range(block_count):
        c = blocks[patch, i]
        row = lax.div(c, row_blocks)
        n = row * row_blocks + lax.rem(c - row * row_blocks + 1, row_blocks)
        averaged = flag[:, i * width : (i + 1) * width] == 1
        at = 0
        for part in parts:
            size = part.shape[0]
            direct = part[:, pl.ds(pl.multiple_of(c * width, width), width)]
            beyond = part[:, pl.ds(pl.multiple_of(n * width, width), width)]
            east = jnp.where(
                lane == width - 1, pltpu.roll(beyond, width - 1, 1), pltpu.roll(direct, width - 1, 1)
            )
            seen[at : at + size, i * width : (i + 1) * width] = jnp.where(
                averaged, 0.5 * (direct + east), direct
            )
            at += size
    at = 0
    for part in parts:
        size = part.shape[0]
        cells[at : at + size, :] = part[:, pl.ds(pl.multiple_of(patch * own_cells, own_cells), own_cells)]
        at += size
    scale = 1.0 / (total - 1.0)
    raw = seen[...]
    seen_mean = jnp.sum(raw, axis=0, keepdims=True) * (1.0 / total)
    offset = raw - seen_mean
    off = split(offset)
    turned = split(offset.T)
    covariance = dot3(turned, off) * scale
    down = lax.broadcasted_iota(jnp.int32, covariance.shape, 0)
    across = lax.broadcasted_iota(jnp.int32, covariance.shape, 1)
    covariance = covariance + jnp.where(down == across, errors[...], 0.0)
    inverse_scale = 1.0 / jnp.sum(jnp.abs(covariance), axis=0, keepdims=True)
    start = ((values[...] - seen_mean) - 0.5 * offset) * inverse_scale
    b1 = covariance * inverse_scale
    s1 = split(b1)
    b2 = 2.0 * b1 - dot3(s1, s1)
    s2 = split(b2)
    b4 = 2.0 * b2 - dot3(s2, s2)
    s4 = split(b4)
    q = start
    for _ in range(3):
        q = start + (q - dot3(split(q), s4))
    q = 2.0 * q - dot3(split(q), s2)
    q = 2.0 * q - dot3(split(q), s1)
    mix = dot3(split(q), off, (((1,), (1,)), ((), ()))) * scale
    state = cells[...]
    shift = state - jnp.sum(state, axis=0, keepdims=True) * (1.0 / total)
    analysed = state + dot3(split(mix), split(shift))
    size = total // groups
    for out, wanted in zip(outs, tops):
        for at, j in enumerate(wanted):
            out[at * size : (at + 1) * size, :] = analysed[j * size : (j + 1) * size, :]


def place_kernel(masks, where, longitudes, *refs):
    sources, out = refs[:-1], refs[-1]
    here = lax.axis_index("mem")
    local = out.shape[0]
    width = sources[0].shape[1]
    found = [sources[where[m][0]][where[m][1] * local : (where[m][1] + 1) * local, :] for m in masks]
    for patch in range(len(masks)):
        value = found[0]
        for m, candidate in zip(masks[1:], found[1:]):
            value = jnp.where((here ^ m) == patch, candidate, value)
        row, column = divmod(patch * width, longitudes)
        out[:, row, column : column + width] = value


def body(
    ensemble,
    diffusivity,
    north_wind,
    observed_blocks,
    eastern_average_flags,
    observed_values,
    observed_error,
):
    local, rows, longitudes = ensemble.shape
    lats, mems = lax.axis_size("lat"), lax.axis_size("mem")
    observations = observed_values.shape[-1]
    cell_count = rows * longitudes
    own_cells = cell_count // mems
    total = local * mems
    near_pairs = xor_pairs(lats, 1)
    far_pairs = [(i, i + 2) for i in range(0, lats - 2, 2)] + [(i, i - 2) for i in range(3, lats, 2)]

    def edges(block):
        if block.shape[1] == 2:
            return block
        return jnp.concatenate([block[:, :2], block[:, -2:]], axis=1)

    pieces = 2
    count = local // pieces
    bits = [1 << k for k in reversed(range(mems.bit_length() - 1))]
    coefficients = edges(jnp.stack([diffusivity, north_wind]))
    near, far = [], []
    for k in range(pieces):
        own = edges(ensemble[k * count : (k + 1) * count])
        if k == 0:
            own = jnp.concatenate([coefficients, own], axis=0)
        near.append(lax.ppermute(own, "lat", near_pairs))
    for k in range(pieces):
        far.append(lax.ppermute(near[k], "lat", far_pairs))
    parts = [[] for _ in range(pieces)]
    for k in range(pieces):
        band = pl.pallas_call(
            functools.partial(forecast_kernel, k * count, count, 2 if k == 0 else 0),
            out_shape=jax.ShapeDtypeStruct((count, cell_count), F32),
            in_specs=[VMEM] * 7,
            out_specs=VMEM,
            cost_estimate=pl.CostEstimate(flops=2000000, bytes_accessed=2000000, transcendentals=0),
            compiler_params=pltpu.CompilerParams(vmem_limit_bytes=8 << 20),
            name="forecast",
        )(ensemble, diffusivity, north_wind, near[k], far[k], near[0], far[0])
        held = [band]
        for bit in bits:
            held = held + [lax.ppermute(a, "mem", xor_pairs(mems, bit)) for a in held]
        parts[k] = held
    masks = [0]
    for bit in bits:
        masks = masks + [m ^ bit for m in masks]

    tops = [[j for j, m in enumerate(masks) if (m & bit) and m < 2 * bit] for bit in bits]
    tops.append([0])
    flat = [parts[k][j] for j in range(mems) for k in range(pieces)]
    shapes = [jax.ShapeDtypeStruct((len(t) * local, own_cells), F32) for t in tops]
    outs = pl.pallas_call(
        functools.partial(gain_kernel, mems, pieces, tops, longitudes),
        out_shape=shapes,
        in_specs=[SMEM] + [VMEM] * (3 + len(flat)),
        out_specs=[VMEM] * len(shapes),
        scratch_shapes=[pltpu.VMEM((total, observations), F32), pltpu.VMEM((total, own_cells), F32)],
        cost_estimate=pl.CostEstimate(flops=5000000000, bytes_accessed=4000000, transcendentals=0),
        compiler_params=pltpu.CompilerParams(vmem_limit_bytes=24 << 20),
        name="gain",
    )(observed_blocks[0], eastern_average_flags[0], observed_values[0], observed_error[0], *flat)
    carried = [(outs[-1], [(0, 0)])]
    for bit, sent, top in zip(bits, outs, tops):
        moving = [(a, g) for a, g in carried if any(left & bit for left, _ in g)]
        moving.append((sent, [(masks[j], 0) for j in top]))
        stay = [(a, [(left if not left & bit else -1, pm) for left, pm in g]) for a, g in carried]
        came = [
            (
                lax.ppermute(a, "mem", xor_pairs(mems, bit)),
                [(left ^ bit if left > 0 and left & bit else -1, pm ^ bit) for left, pm in g],
            )
            for a, g in moving
        ]
        carried = stay + came
    where = {}
    for index, (_, g) in enumerate(carried):
        for at, (left, pm) in enumerate(g):
            if left == 0:
                where[pm] = (index, at)
    return pl.pallas_call(
        functools.partial(place_kernel, masks, where, longitudes),
        out_shape=jax.ShapeDtypeStruct((local, rows, longitudes), F32),
        in_specs=[VMEM] * len(carried),
        out_specs=VMEM,
        cost_estimate=pl.CostEstimate(flops=100000, bytes_accessed=600000, transcendentals=0),
        compiler_params=pltpu.CompilerParams(vmem_limit_bytes=8 << 20),
        name="place",
    )(*[a for a, _ in carried])


def solution(mesh):
    return jax.shard_map(
        body,
        mesh=mesh,
        in_specs=(
            P("mem", "lat", None),
            P("lat", None),
            P("lat", None),
            P("lat", None, None),
            P("lat", None, None),
            P("lat", "mem", None),
            P("lat", "mem", None),
        ),
        out_specs=P("mem", "lat", None),
        check_vma=False,
    )
```

```python
import functools

import jax
import jax.numpy as jnp
from jax import lax
from jax.experimental import pallas as pl
from jax.experimental.pallas import tpu as pltpu
from jax.sharding import PartitionSpec as P

NEWTON = 4
ADVECTION = 0.1
F32 = jnp.float32
BF16 = jnp.bfloat16
VMEM = pl.BlockSpec(memory_space=pltpu.VMEM)
SMEM = pl.BlockSpec(memory_space=pltpu.SMEM)


def xor_pairs(count, bit):
    return [(i, i ^ bit) for i in range(count)]


def piece_counts(local):
    unit = 8 if local % 8 == 0 else 1
    whole = local // unit
    first = (whole + 1) // 2
    return [n * unit for n in (first, whole - first) if n]


def step(rows, diffusivity, north_wind):
    out = []
    for r in range(1, len(rows) - 1):
        north, centre, south = rows[r - 1], rows[r], rows[r + 1]
        last = centre.shape[1] - 1
        eastern = pltpu.roll(centre, last, 1)
        western = pltpu.roll(centre, 1, 1)
        out.append(
            centre
            - ADVECTION * centre * (eastern - western)
            - north_wind[r - 1] * (south - north)
            + diffusivity[r - 1] * (eastern + western + north + south - 4.0 * centre)
        )
    return out


def forecast_kernel(lats, first, count, lead, own, dif, wind, near, far, coef_near, coef_far, *tables_and_out):
    out = tables_and_out[-1]
    place = lax.axis_index("lat")
    even = lax.rem(place, 2) == 0
    inner = (place > 0) & (place < lats - 1)
    rows, longitudes = own.shape[1], own.shape[2]
    edge = near.shape[1]

    def pick(a, b):
        return jnp.where(even, a, b)

    def members(ref, r):
        return ref[lead : lead + count, r, :]

    def beyond(x):
        return jnp.where(inner, x, 0.0)

    low = [pick(beyond(members(far, r)), members(near, r)) for r in (edge - 2, edge - 1)]
    high = [pick(members(near, r), beyond(members(far, r))) for r in (0, 1)]
    here = [own[first : first + count, r, :] for r in range(rows)]

    def coefficient(which, ref):
        before = pick(beyond(coef_far[which : which + 1, edge - 1, :]), coef_near[which : which + 1, edge - 1, :])
        after = pick(coef_near[which : which + 1, 0, :], beyond(coef_far[which : which + 1, 0, :]))
        return [before] + [ref[r : r + 1, :] for r in range(rows)] + [after]

    d, w = coefficient(0, dif), coefficient(1, wind)
    once = step(low + here + high, d, w)
    twice = step(once, d[1:-1], w[1:-1])
    for r in range(rows):
        out[:, r * longitudes : (r + 1) * longitudes] = twice[r]


def split(x):
    high = x.astype(BF16)
    return high, (x - high.astype(F32)).astype(BF16)


def dot3(a, b, dims=(((1,), (0,)), ((), ()))):
    mul = functools.partial(lax.dot_general, dimension_numbers=dims, preferred_element_type=F32)
    return mul(a[0], b[0]) + (mul(a[0], b[1]) + mul(a[1], b[0]))


def gain_kernel(groups, pieces, longitudes, blocks, flags, values, errors, *refs):
    parts = refs[: groups * pieces]
    outs = refs[groups * pieces : -2]
    seen, cells = refs[-2:]
    patch = lax.axis_index("mem")
    total, observations = seen.shape
    own_cells = cells.shape[1]
    block_count = blocks.shape[1]
    width = observations // block_count
    row_blocks = longitudes // width
    flag = flags[pl.ds(patch, 1), :]
    lane = lax.broadcasted_iota(jnp.int32, (1, width), 1)
    for i in range(block_count):
        c = blocks[patch, i]
        row = lax.div(c, row_blocks)
        n = row * row_blocks + lax.rem(c - row * row_blocks + 1, row_blocks)
        averaged = flag[:, i * width : (i + 1) * width] == 1
        at = 0
        for part in parts:
            size = part.shape[0]
            direct = part[:, pl.ds(pl.multiple_of(c * width, width), width)]
            beyond = part[:, pl.ds(pl.multiple_of(n * width, width), width)]
            east = jnp.where(
                lane == width - 1, pltpu.roll(beyond, width - 1, 1), pltpu.roll(direct, width - 1, 1)
            )
            seen[at : at + size, i * width : (i + 1) * width] = jnp.where(
                averaged, 0.5 * (direct + east), direct
            )
            at += size
    at = 0
    for part in parts:
        size = part.shape[0]
        cells[at : at + size, :] = part[:, pl.ds(pl.multiple_of(patch * own_cells, own_cells), own_cells)]
        at += size
    scale = 1.0 / (total - 1.0)
    raw = seen[...]
    seen_mean = jnp.sum(raw, axis=0, keepdims=True) * (1.0 / total)
    offset = raw - seen_mean
    off = split(offset)
    turned = split(offset.T)
    covariance = dot3(turned, off) * scale
    down = lax.broadcasted_iota(jnp.int32, covariance.shape, 0)
    across = lax.broadcasted_iota(jnp.int32, covariance.shape, 1)
    covariance = covariance + jnp.where(down == across, errors[...], 0.0)
    inverse_scale = 1.0 / jnp.sum(jnp.abs(covariance), axis=0, keepdims=True)
    start = ((values[...] - seen_mean) - 0.5 * offset) * inverse_scale
    b1 = covariance * inverse_scale
    s1 = split(b1)
    b2 = 2.0 * b1 - dot3(s1, s1)
    s2 = split(b2)
    b4 = 2.0 * b2 - dot3(s2, s2)
    s4 = split(b4)
    q = start
    for _ in range(3):
        q = start + (q - dot3(split(q), s4))
    q = 2.0 * q - dot3(split(q), s2)
    q = 2.0 * q - dot3(split(q), s1)
    mix = dot3(split(q), off, (((1,), (1,)), ((), ()))) * scale
    state = cells[...]
    shift = state - jnp.sum(state, axis=0, keepdims=True) * (1.0 / total)
    analysed = state + dot3(split(mix), split(shift))
    size = total // groups
    for j, out in enumerate(outs):
        out[...] = analysed[j * size : (j + 1) * size, :]


def place_kernel(masks, longitudes, *refs):
    sources, out = refs[:-1], refs[-1]
    here = lax.axis_index("mem")
    width = sources[0].shape[1]
    found = [source[...] for source in sources]
    for patch in range(len(masks)):
        value = found[0]
        for m, candidate in zip(masks[1:], found[1:]):
            value = jnp.where((here ^ m) == patch, candidate, value)
        row, column = divmod(patch * width, longitudes)
        out[:, row, column : column + width] = value


def body(
    ensemble,
    diffusivity,
    north_wind,
    observed_blocks,
    eastern_average_flags,
    observed_values,
    observed_error,
):
    local, rows, longitudes = ensemble.shape
    lats, mems = lax.axis_size("lat"), lax.axis_size("mem")
    observations = observed_values.shape[-1]
    cell_count = rows * longitudes
    own_cells = cell_count // mems
    total = local * mems
    near_pairs = xor_pairs(lats, 1)
    far_pairs = [(i, i + 2) for i in range(0, lats - 2, 2)] + [(i, i - 2) for i in range(3, lats, 2)]
    far_pairs += [(lats - 2, lats - 1), (1, 0)]

    def edges(block):
        if block.shape[1] == 2:
            return block
        return jnp.concatenate([block[:, :2], block[:, -2:]], axis=1)

    counts = piece_counts(local)
    pieces = len(counts)
    firsts = [sum(counts[:k]) for k in range(pieces)]
    bits = [1 << k for k in reversed(range(mems.bit_length() - 1))]
    coefficients = edges(jnp.stack([diffusivity, north_wind]))
    near, far = [], []
    for k in range(pieces):
        own = edges(ensemble[firsts[k] : firsts[k] + counts[k]])
        if k == 0:
            own = jnp.concatenate([coefficients, own], axis=0)
        near.append(lax.ppermute(own, "lat", near_pairs))
    for k in range(pieces):
        far.append(lax.ppermute(near[k], "lat", far_pairs))
    tables = observed_blocks[0], eastern_average_flags[0], observed_values[0], observed_error[0]
    parts = [[] for _ in range(pieces)]
    for k in range(pieces):
        band = pl.pallas_call(
            functools.partial(forecast_kernel, lats, firsts[k], counts[k], 2 if k == 0 else 0),
            out_shape=jax.ShapeDtypeStruct((counts[k], cell_count), F32),
            in_specs=[VMEM] * (7 + len(tables)),
            out_specs=VMEM,
            cost_estimate=pl.CostEstimate(flops=2000000, bytes_accessed=2000000, transcendentals=0),
            compiler_params=pltpu.CompilerParams(vmem_limit_bytes=8 << 20),
            name="forecast",
        )(ensemble, diffusivity, north_wind, near[k], far[k], near[0], far[0], *tables)
        held = [band]
        for bit in bits:
            held = held + [lax.ppermute(a, "mem", xor_pairs(mems, bit)) for a in held]
        parts[k] = held
    masks = [0]
    for bit in bits:
        masks = masks + [m ^ bit for m in masks]

    flat = [parts[k][j] for j in range(mems) for k in range(pieces)]
    shapes = [jax.ShapeDtypeStruct((local, own_cells), F32) for _ in masks]
    outs = pl.pallas_call(
        functools.partial(gain_kernel, mems, pieces, longitudes),
        out_shape=shapes,
        in_specs=[SMEM] + [VMEM] * (3 + len(flat)),
        out_specs=[VMEM] * len(shapes),
        scratch_shapes=[pltpu.VMEM((total, observations), F32), pltpu.VMEM((total, own_cells), F32)],
        cost_estimate=pl.CostEstimate(flops=5000000000, bytes_accessed=4000000, transcendentals=0),
        compiler_params=pltpu.CompilerParams(vmem_limit_bytes=24 << 20),
        name="gain",
    )(*tables, *flat)
    came = {0: outs[0]}
    for mask in sorted(masks[1:], reverse=True):
        pairs = [(i, i ^ mask) for i in range(mems)]
        came[mask] = lax.ppermute(outs[masks.index(mask)], "mem", pairs)
    return pl.pallas_call(
        functools.partial(place_kernel, masks, longitudes),
        out_shape=jax.ShapeDtypeStruct((local, rows, longitudes), F32),
        in_specs=[VMEM] * mems,
        out_specs=VMEM,
        cost_estimate=pl.CostEstimate(flops=100000, bytes_accessed=600000, transcendentals=0),
        compiler_params=pltpu.CompilerParams(vmem_limit_bytes=8 << 20),
        name="place",
    )(*[came[m] for m in masks])


def solution(mesh):
    return jax.shard_map(
        body,
        mesh=mesh,
        in_specs=(
            P("mem", "lat", None),
            P("lat", None),
            P("lat", None),
            P("lat", None, None),
            P("lat", None, None),
            P("lat", "mem", None),
            P("lat", "mem", None),
        ),
        out_specs=P("mem", "lat", None),
        check_vma=False,
    )
```

```python
import functools

import jax
import jax.numpy as jnp
from jax import lax
from jax.experimental import pallas as pl
from jax.experimental.pallas import tpu as pltpu
from jax.sharding import PartitionSpec as P


ADVECTION = 0.1
F32 = jnp.float32
BF16 = jnp.bfloat16
VMEM = pl.BlockSpec(memory_space=pltpu.VMEM)
SMEM = pl.BlockSpec(memory_space=pltpu.SMEM)


def xor_pairs(count, bit):
    return [(i, i ^ bit) for i in range(count)]


def piece_counts(local):
    unit = 8 if local % 8 == 0 else 1
    whole = local // unit
    first = (whole + 1) // 2
    return [n * unit for n in (first, whole - first) if n]


def step(rows, diffusivity, north_wind):
    out = []
    for r in range(1, len(rows) - 1):
        north, centre, south = rows[r - 1], rows[r], rows[r + 1]
        last = centre.shape[1] - 1
        eastern = pltpu.roll(centre, last, 1)
        western = pltpu.roll(centre, 1, 1)
        out.append(
            centre
            - ADVECTION * centre * (eastern - western)
            - north_wind[r - 1] * (south - north)
            + diffusivity[r - 1] * (eastern + western + north + south - 4.0 * centre)
        )
    return out


def forecast_kernel(lats, first, count, lead, own, dif, wind, near, far, coef_near, coef_far, *tables_and_out):
    out = tables_and_out[-1]
    place = lax.axis_index("lat")
    even = lax.rem(place, 2) == 0
    inner = (place > 0) & (place < lats - 1)
    rows, longitudes = own.shape[1], own.shape[2]
    edge = near.shape[1]

    def pick(a, b):
        return jnp.where(even, a, b)

    def members(ref, r):
        return ref[lead : lead + count, r, :]

    def beyond(x):
        return jnp.where(inner, x, 0.0)

    low = [pick(beyond(members(far, r)), members(near, r)) for r in (edge - 2, edge - 1)]
    high = [pick(members(near, r), beyond(members(far, r))) for r in (0, 1)]
    here = [own[first : first + count, r, :] for r in range(rows)]

    def coefficient(which, ref):
        before = pick(beyond(coef_far[which : which + 1, edge - 1, :]), coef_near[which : which + 1, edge - 1, :])
        after = pick(coef_near[which : which + 1, 0, :], beyond(coef_far[which : which + 1, 0, :]))
        return [before] + [ref[r : r + 1, :] for r in range(rows)] + [after]

    d, w = coefficient(0, dif), coefficient(1, wind)
    once = step(low + here + high, d, w)
    twice = step(once, d[1:-1], w[1:-1])
    for r in range(rows):
        out[:, r * longitudes : (r + 1) * longitudes] = twice[r]


def split(x):
    high = x.astype(BF16)
    return high, (x - high.astype(F32)).astype(BF16)


def dot3(a, b, width=256):
    rows = a[0].shape[0]
    mul = functools.partial(jnp.dot, preferred_element_type=F32)
    stacked = jnp.concatenate(a, axis=0)
    out = []
    for at in range(0, b[0].shape[1], width):
        both = mul(stacked, b[0][:, at : at + width])
        out.append(both[:rows] + (both[rows:] + mul(a[0], b[1][:, at : at + width])))
    return jnp.concatenate(out, axis=1)


def dot1(a, b, width=256):
    mul = functools.partial(jnp.dot, preferred_element_type=F32)
    return jnp.concatenate([mul(a, b[:, at : at + width]) for at in range(0, b.shape[1], width)], axis=1)


def observe(parts, longitudes, own_cells, blocks, flags):
    patch = lax.axis_index("mem")
    block_count = blocks.shape[1]
    width = flags.shape[1] // block_count
    row_blocks = longitudes // width
    flag = flags[pl.ds(patch, 1), :]
    lane = lax.broadcasted_iota(jnp.int32, (1, width), 1)
    columns = []
    for i in range(block_count):
        c = blocks[patch, i]
        row = lax.div(c, row_blocks)
        n = row * row_blocks + lax.rem(c - row * row_blocks + 1, row_blocks)
        averaged = flag[:, i * width : (i + 1) * width] == 1
        values = []
        for part in parts:
            direct = part[:, pl.ds(pl.multiple_of(c * width, width), width)]
            beyond = part[:, pl.ds(pl.multiple_of(n * width, width), width)]
            east = pltpu.roll(jnp.where(lane == 0, beyond, direct), width - 1, 1)
            values.append(jnp.where(averaged, 0.5 * (direct + east), direct))
        columns.append(jnp.concatenate(values, axis=0))
    return jnp.concatenate(columns, axis=1), own(parts, own_cells)


def own(parts, own_cells):
    at = pl.multiple_of(lax.axis_index("mem") * own_cells, own_cells)
    return jnp.concatenate([part[:, pl.ds(at, own_cells)] for part in parts], axis=0)


def doubled(x):
    high, low = split(x)
    return jnp.concatenate([high, high, low, low], axis=0)


def moments(seen, cells, before, count):
    if before is None:
        seen_mean = jnp.sum(seen, axis=0, keepdims=True) * (1.0 / count)
        cell_mean = jnp.sum(cells, axis=0, keepdims=True) * (1.0 / count)
        left = seen - seen_mean
        right, right_cells = left, cells - cell_mean
    else:
        left, right_cells = seen - before[0], cells - before[1]
        shift = jnp.sum(left, axis=0, keepdims=True) * (1.0 / count)
        cell_shift = jnp.sum(right_cells, axis=0, keepdims=True) * (1.0 / count)
        seen_mean, cell_mean = before[0] + shift, before[1] + cell_shift
        right, right_cells = left - shift, right_cells - cell_shift
    turned = jnp.concatenate(split(left), axis=0).T
    turned = jnp.concatenate([turned, turned], axis=1)
    return dot1(turned, doubled(right)), dot1(turned, doubled(right_cells)), seen_mean, cell_mean


def moment_kernel(has_before, count, longitudes, blocks, flags, *refs):
    refs = list(refs)
    outs = refs[-5:]
    before = refs[:4] if has_before else None
    parts = refs[4 if has_before else 0 : -5]
    seen, cells = observe(parts, longitudes, outs[1].shape[1], blocks, flags)
    means = None if before is None else (before[2][...], before[3][...])
    square, cross, seen_mean, cell_mean = moments(seen, cells, means, count)
    if before is not None:
        square, cross = square + before[0][...], cross + before[1][...]
    for out, value in zip(outs, (square, cross, seen_mean, cell_mean, seen)):
        out[...] = value


def gain_kernel(earlier, last, order, longitudes, blocks, flags, values, errors, *refs):
    cov, outs = refs[-1], refs[-1 - (1 + max(j for j, _ in order)) : -1]
    before, first_seen, parts = refs[:4], refs[4 : 4 + earlier], refs[4 + earlier : 4 + earlier + len(order)]
    own_cells = outs[0].shape[1]
    total = sum(part.shape[0] for part in parts)
    scale = 1.0 / (total - 1.0)
    last_seen, last_cells = observe(parts[-last:], longitudes, own_cells, blocks, flags)
    square, cross, seen_mean, _ = moments(last_seen, last_cells, (before[2][...], before[3][...]), total)
    cross = split((cross + before[1][...]) * scale)
    cov[...] = (square + before[0][...]) * scale
    tile = 128
    down = lax.broadcasted_iota(jnp.int32, (tile, tile), 0)
    across = lax.broadcasted_iota(jnp.int32, (tile, tile), 1)
    for at in range(0, cov.shape[0], tile):
        here = slice(at, at + tile)
        cov[here, here] += jnp.where(down == across, errors[:, here], 0.0)
    covariance = cov[...]
    inverse_scale = 1.0 / jnp.sum(jnp.abs(covariance), axis=0, keepdims=True)
    seen = jnp.concatenate([ref[...] for ref in first_seen] + [last_seen], axis=0)
    start = ((values[...] - seen_mean) - 0.5 * (seen - seen_mean)) * inverse_scale
    b1 = covariance * inverse_scale
    s1 = split(b1)
    b2 = 2.0 * b1 - dot3(s1, s1)
    s2 = split(b2)
    b4 = 2.0 * b2 - dot3(s2, s2)
    s4 = split(b4)
    q = start + (start - dot1(start.astype(BF16), s4[0]))
    for _ in range(2):
        q = start + (q - dot3(split(q), s4))
    q = 2.0 * q - dot3(split(q), s2)
    q = 2.0 * q - dot3(split(q), s1)
    update = dot3(split(q), cross)
    at = 0
    for part, (j, row) in zip(parts, order):
        size = part.shape[0]
        outs[j][row : row + size, :] = own([part], own_cells) + update[at : at + size, :]
        at += size


def place_kernel(masks, longitudes, *refs):
    sources, out = refs[:-1], refs[-1]
    here = lax.axis_index("mem")
    width = sources[0].shape[1]
    found = [source[...] for source in sources]
    for patch in range(len(masks)):
        value = found[0]
        for m, candidate in zip(masks[1:], found[1:]):
            value = jnp.where((here ^ m) == patch, candidate, value)
        row, column = divmod(patch * width, longitudes)
        out[:, row, column : column + width] = value


def body(
    ensemble,
    diffusivity,
    north_wind,
    observed_blocks,
    eastern_average_flags,
    observed_values,
    observed_error,
):
    local, rows, longitudes = ensemble.shape
    lats, mems = lax.axis_size("lat"), lax.axis_size("mem")
    observations = observed_values.shape[-1]
    cell_count = rows * longitudes
    own_cells = cell_count // mems
    near_pairs = xor_pairs(lats, 1)
    far_pairs = [(i, i + 2) for i in range(0, lats - 2, 2)] + [(i, i - 2) for i in range(3, lats, 2)]
    far_pairs += [(lats - 2, lats - 1), (1, 0)]

    def edges(block):
        if block.shape[1] == 2:
            return block
        return jnp.concatenate([block[:, :2], block[:, -2:]], axis=1)

    counts = piece_counts(local)
    pieces = len(counts)
    firsts = [sum(counts[:k]) for k in range(pieces)]
    bits = [1 << k for k in reversed(range(mems.bit_length() - 1))]
    coefficients = edges(jnp.stack([diffusivity, north_wind]))
    near, far = [], []
    for k in range(pieces):
        own = edges(ensemble[firsts[k] : firsts[k] + counts[k]])
        if k == 0:
            own = jnp.concatenate([coefficients, own], axis=0)
        near.append(lax.ppermute(own, "lat", near_pairs))
    for k in range(pieces):
        far.append(lax.ppermute(near[k], "lat", far_pairs))
    tables = observed_blocks[0], eastern_average_flags[0], observed_values[0], observed_error[0]
    top, low_bits = bits[0], bits[1:]

    def spread(a):
        held = [a]
        for bit in low_bits:
            held = held + [lax.ppermute(b, "mem", xor_pairs(mems, bit)) for b in held]
        return held

    masks = [0]
    for bit in low_bits:
        masks = masks + [m ^ bit for m in masks]
    masks = masks + [m ^ top for m in masks]
    near_half, far_half = [], []
    for k in range(pieces):
        band = pl.pallas_call(
            functools.partial(forecast_kernel, lats, firsts[k], counts[k], 2 if k == 0 else 0),
            out_shape=jax.ShapeDtypeStruct((counts[k], cell_count), F32),
            in_specs=[VMEM] * (7 + len(tables)),
            out_specs=VMEM,
            cost_estimate=pl.CostEstimate(flops=2000000, bytes_accessed=2000000, transcendentals=0),
            compiler_params=pltpu.CompilerParams(vmem_limit_bytes=8 << 20),
        )(ensemble, diffusivity, north_wind, near[k], far[k], near[0], far[0], *tables)
        far_half.append(lax.ppermute(band, "mem", xor_pairs(mems, top)))
        near_half.append(spread(band))

    def add_moments(stage, before, count):
        members = sum(a.shape[0] for a in stage)
        *after, stage_seen = pl.pallas_call(
            functools.partial(moment_kernel, len(before) > 0, count + members, longitudes),
            out_shape=[
                jax.ShapeDtypeStruct((observations, observations), F32),
                jax.ShapeDtypeStruct((observations, own_cells), F32),
                jax.ShapeDtypeStruct((1, observations), F32),
                jax.ShapeDtypeStruct((1, own_cells), F32),
                jax.ShapeDtypeStruct((members, observations), F32),
            ],
            in_specs=[SMEM] + [VMEM] * (1 + len(before) + len(stage)),
            out_specs=[VMEM] * 5,
            cost_estimate=pl.CostEstimate(flops=800000000, bytes_accessed=3000000, transcendentals=0),
            compiler_params=pltpu.CompilerParams(vmem_limit_bytes=16 << 20),
        )(*tables[:2], *before, *stage)
        return after, stage_seen

    stage = [near_half[k][j] for k in range(pieces) for j in range(mems // 2)]
    flat, order = stage, [(j, firsts[k]) for k in range(pieces) for j in range(mems // 2)]
    before, stage_seen = add_moments(stage, (), 0)
    seen = [stage_seen]
    for k in range(pieces):
        stage = spread(far_half[k])
        if k < pieces - 1:
            before, stage_seen = add_moments(stage, before, sum(a.shape[0] for a in flat))
            seen.append(stage_seen)
        flat = flat + stage
        order = order + [(j, firsts[k]) for j in range(mems // 2, mems)]
    outs = pl.pallas_call(
        functools.partial(
            gain_kernel, len(seen), len(stage), order, longitudes
        ),
        out_shape=[jax.ShapeDtypeStruct((local, own_cells), F32) for _ in masks],
        in_specs=[SMEM] + [VMEM] * (3 + len(before) + len(seen) + len(flat)),
        out_specs=[VMEM] * mems,
        scratch_shapes=[pltpu.VMEM((observations, observations), F32)],
        cost_estimate=pl.CostEstimate(flops=5000000000, bytes_accessed=4000000, transcendentals=0),
        compiler_params=pltpu.CompilerParams(vmem_limit_bytes=24 << 20),
        name="gain",
    )(*tables, *before, *seen, *flat)
    came = {0: outs[0]}
    for mask in sorted(masks[1:], reverse=True):
        pairs = [(i, i ^ mask) for i in range(mems)]
        came[mask] = lax.ppermute(outs[masks.index(mask)], "mem", pairs)
    return pl.pallas_call(
        functools.partial(place_kernel, masks, longitudes),
        out_shape=jax.ShapeDtypeStruct((local, rows, longitudes), F32),
        in_specs=[VMEM] * mems,
        out_specs=VMEM,
        cost_estimate=pl.CostEstimate(flops=100000, bytes_accessed=600000, transcendentals=0),
        compiler_params=pltpu.CompilerParams(vmem_limit_bytes=8 << 20),
        name="place",
    )(*[came[m] for m in masks])


def solution(mesh):
    return jax.shard_map(
        body,
        mesh=mesh,
        in_specs=(
            P("mem", "lat", None),
            P("lat", None),
            P("lat", None),
            P("lat", None, None),
            P("lat", None, None),
            P("lat", "mem", None),
            P("lat", "mem", None),
        ),
        out_specs=P("mem", "lat", None),
        check_vma=False,
    )
```

```python
import functools

import jax
import jax.numpy as jnp
from jax import lax
from jax.experimental import pallas as pl
from jax.experimental.pallas import tpu as pltpu
from jax.sharding import PartitionSpec as P


ADVECTION = 0.1
F32 = jnp.float32
BF16 = jnp.bfloat16
VMEM = pl.BlockSpec(memory_space=pltpu.VMEM)
SMEM = pl.BlockSpec(memory_space=pltpu.SMEM)


def xor_pairs(count, bit):
    return [(i, i ^ bit) for i in range(count)]


def piece_counts(local):
    unit = 8 if local % 8 == 0 else 1
    whole = local // unit
    first = (whole + 1) // 2
    return [n * unit for n in (first, whole - first) if n]


def step(rows, diffusivity, north_wind):
    out = []
    for r in range(1, len(rows) - 1):
        north, centre, south = rows[r - 1], rows[r], rows[r + 1]
        last = centre.shape[1] - 1
        eastern = pltpu.roll(centre, last, 1)
        western = pltpu.roll(centre, 1, 1)
        out.append(
            centre
            - ADVECTION * centre * (eastern - western)
            - north_wind[r - 1] * (south - north)
            + diffusivity[r - 1] * (eastern + western + north + south - 4.0 * centre)
        )
    return out


def forecast_kernel(lats, first, count, lead, own, dif, wind, near, far, coef_near, coef_far, *tables_and_out):
    out = tables_and_out[-1]
    place = lax.axis_index("lat")
    even = lax.rem(place, 2) == 0
    inner = (place > 0) & (place < lats - 1)
    rows, longitudes = own.shape[1], own.shape[2]
    edge = near.shape[1]

    def pick(a, b):
        return jnp.where(even, a, b)

    def members(ref, r):
        return ref[lead : lead + count, r, :]

    def beyond(x):
        return jnp.where(inner, x, 0.0)

    low = [pick(beyond(members(far, r)), members(near, r)) for r in (edge - 2, edge - 1)]
    high = [pick(members(near, r), beyond(members(far, r))) for r in (0, 1)]
    here = [own[first : first + count, r, :] for r in range(rows)]

    def coefficient(which, ref):
        before = pick(beyond(coef_far[which : which + 1, edge - 1, :]), coef_near[which : which + 1, edge - 1, :])
        after = pick(coef_near[which : which + 1, 0, :], beyond(coef_far[which : which + 1, 0, :]))
        return [before] + [ref[r : r + 1, :] for r in range(rows)] + [after]

    d, w = coefficient(0, dif), coefficient(1, wind)
    once = step(low + here + high, d, w)
    twice = step(once, d[1:-1], w[1:-1])
    for r in range(rows):
        out[:, r * longitudes : (r + 1) * longitudes] = twice[r]


def split(x):
    high = x.astype(BF16)
    return high, (x - high.astype(F32)).astype(BF16)


def dot3(a, b, width=256):
    rows = a[0].shape[0]
    mul = functools.partial(jnp.dot, preferred_element_type=F32)
    stacked = jnp.concatenate(a, axis=0)
    out = []
    for at in range(0, b[0].shape[1], width):
        both = mul(stacked, b[0][:, at : at + width])
        out.append(both[:rows] + (both[rows:] + mul(a[0], b[1][:, at : at + width])))
    return jnp.concatenate(out, axis=1)


def dot1(a, b, width=256):
    mul = functools.partial(jnp.dot, preferred_element_type=F32)
    return jnp.concatenate([mul(a, b[:, at : at + width]) for at in range(0, b.shape[1], width)], axis=1)


def observe(parts, longitudes, own_cells, blocks, flags):
    patch = lax.axis_index("mem")
    block_count = blocks.shape[1]
    width = flags.shape[1] // block_count
    row_blocks = longitudes // width
    flag = flags[pl.ds(patch, 1), :]
    lane = lax.broadcasted_iota(jnp.int32, (1, width), 1)
    columns = []
    for i in range(block_count):
        c = blocks[patch, i]
        row = lax.div(c, row_blocks)
        n = row * row_blocks + lax.rem(c - row * row_blocks + 1, row_blocks)
        averaged = flag[:, i * width : (i + 1) * width] == 1
        values = []
        for part in parts:
            direct = part[:, pl.ds(pl.multiple_of(c * width, width), width)]
            beyond = part[:, pl.ds(pl.multiple_of(n * width, width), width)]
            east = pltpu.roll(jnp.where(lane == 0, beyond, direct), width - 1, 1)
            values.append(jnp.where(averaged, 0.5 * (direct + east), direct))
        columns.append(jnp.concatenate(values, axis=0))
    return jnp.concatenate(columns, axis=1), own(parts, own_cells)


def own(parts, own_cells):
    at = pl.multiple_of(lax.axis_index("mem") * own_cells, own_cells)
    return jnp.concatenate([part[:, pl.ds(at, own_cells)] for part in parts], axis=0)


def doubled(x):
    high, low = split(x)
    return jnp.concatenate([high, high, low, low], axis=0)


def moments(seen, cells, before, count):
    if before is None:
        seen_mean = jnp.sum(seen, axis=0, keepdims=True) * (1.0 / count)
        cell_mean = jnp.sum(cells, axis=0, keepdims=True) * (1.0 / count)
        left = seen - seen_mean
        right, right_cells = left, cells - cell_mean
    else:
        left, right_cells = seen - before[0], cells - before[1]
        shift = jnp.sum(left, axis=0, keepdims=True) * (1.0 / count)
        cell_shift = jnp.sum(right_cells, axis=0, keepdims=True) * (1.0 / count)
        seen_mean, cell_mean = before[0] + shift, before[1] + cell_shift
        right, right_cells = left - shift, right_cells - cell_shift
    turned = jnp.concatenate(split(left), axis=0).T
    turned = jnp.concatenate([turned, turned], axis=1)
    return dot1(turned, doubled(right)), dot1(turned, doubled(right_cells)), seen_mean, cell_mean


def moment_kernel(has_before, count, longitudes, blocks, flags, *refs):
    refs = list(refs)
    outs = refs[-5:]
    before = refs[:4] if has_before else None
    parts = refs[4 if has_before else 0 : -5]
    seen, cells = observe(parts, longitudes, outs[1].shape[1], blocks, flags)
    means = None if before is None else (before[2][...], before[3][...])
    square, cross, seen_mean, cell_mean = moments(seen, cells, means, count)
    if before is not None:
        square, cross = square + before[0][...], cross + before[1][...]
    for out, value in zip(outs, (square, cross, seen_mean, cell_mean, seen)):
        out[...] = value


def square(x):
    half = x[0].shape[0] // 2
    first, second = slice(0, half), slice(half, 2 * half)

    def block(rows, columns):
        mul = functools.partial(jnp.dot, preferred_element_type=F32)
        (high, low), (high_right, low_right) = [p[rows] for p in x], [p[:, columns] for p in x]
        quarter = half // 2
        out = []
        for at in (0, quarter):
            h, l = high[at : at + quarter], low[at : at + quarter]
            both = mul(jnp.concatenate([h, l], axis=0), high_right)
            out.append(both[:quarter] + (both[quarter:] + mul(h, low_right)))
        return jnp.concatenate(out, axis=0)

    corner = block(first, second)
    above = jnp.concatenate([block(first, first), corner], axis=1)
    below = jnp.concatenate([corner.T, block(second, second)], axis=1)
    return jnp.concatenate([above, below], axis=0)


def gain_kernel(earlier, last, order, longitudes, blocks, flags, values, errors, *refs):
    cov, outs = refs[-1], refs[-1 - (1 + max(j for j, _ in order)) : -1]
    before, first_seen, parts = refs[:4], refs[4 : 4 + earlier], refs[4 + earlier : 4 + earlier + len(order)]
    own_cells = outs[0].shape[1]
    total = sum(part.shape[0] for part in parts)
    last_seen, last_cells = observe(parts[-last:], longitudes, own_cells, blocks, flags)
    square_sum, cross, seen_mean, _ = moments(last_seen, last_cells, (before[2][...], before[3][...]), total)
    cov[...] = square_sum + before[0][...]
    tile = 128
    down = lax.broadcasted_iota(jnp.int32, (tile, tile), 0)
    across = lax.broadcasted_iota(jnp.int32, (tile, tile), 1)
    for at in range(0, cov.shape[0], tile):
        here = slice(at, at + tile)
        cov[here, here] += jnp.where(down == across, errors[:, here] * (total - 1.0), 0.0)
    covariance = cov[...]
    size = jnp.abs(covariance)
    root = lax.rsqrt(jnp.sum(size, axis=0, keepdims=True))
    root_down = lax.rsqrt(jnp.sum(size, axis=1, keepdims=True))
    cross = split((cross + before[1][...]) * root_down)
    seen = jnp.concatenate([ref[...] for ref in first_seen] + [last_seen], axis=0)
    start = ((values[...] - seen_mean) - 0.5 * (seen - seen_mean)) * root
    b1 = (covariance * root_down) * root
    s1 = split(b1)
    b2 = 2.0 * b1 - square(s1)
    s2 = split(b2)
    b4 = 2.0 * b2 - square(s2)
    s4 = split(b4)
    q = start + (start - dot1(start.astype(BF16), s4[0]))
    for _ in range(2):
        q = start + (q - dot3(split(q), s4))
    q = 2.0 * q - dot3(split(q), s2)
    q = 2.0 * q - dot3(split(q), s1)
    update = dot3(split(q), cross)
    at = 0
    for part, (j, row) in zip(parts, order):
        size = part.shape[0]
        outs[j][row : row + size, :] = own([part], own_cells) + update[at : at + size, :]
        at += size


def place_kernel(masks, longitudes, *refs):
    sources, out = refs[:-1], refs[-1]
    here = lax.axis_index("mem")
    width = sources[0].shape[1]
    found = [source[...] for source in sources]
    for patch in range(len(masks)):
        value = found[0]
        for m, candidate in zip(masks[1:], found[1:]):
            value = jnp.where((here ^ m) == patch, candidate, value)
        row, column = divmod(patch * width, longitudes)
        out[:, row, column : column + width] = value


def body(
    ensemble,
    diffusivity,
    north_wind,
    observed_blocks,
    eastern_average_flags,
    observed_values,
    observed_error,
):
    local, rows, longitudes = ensemble.shape
    lats, mems = lax.axis_size("lat"), lax.axis_size("mem")
    observations = observed_values.shape[-1]
    cell_count = rows * longitudes
    own_cells = cell_count // mems
    near_pairs = xor_pairs(lats, 1)
    far_pairs = [(i, i + 2) for i in range(0, lats - 2, 2)] + [(i, i - 2) for i in range(3, lats, 2)]
    far_pairs += [(lats - 2, lats - 1), (1, 0)]

    def edges(block):
        if block.shape[1] == 2:
            return block
        return jnp.concatenate([block[:, :2], block[:, -2:]], axis=1)

    counts = piece_counts(local)
    pieces = len(counts)
    firsts = [sum(counts[:k]) for k in range(pieces)]
    bits = [1 << k for k in reversed(range(mems.bit_length() - 1))]
    coefficients = edges(jnp.stack([diffusivity, north_wind]))
    near, far = [], []
    for k in range(pieces):
        own = edges(ensemble[firsts[k] : firsts[k] + counts[k]])
        if k == 0:
            own = jnp.concatenate([coefficients, own], axis=0)
        near.append(lax.ppermute(own, "lat", near_pairs))
    for k in range(pieces):
        far.append(lax.ppermute(near[k], "lat", far_pairs))
    tables = observed_blocks[0], eastern_average_flags[0], observed_values[0], observed_error[0]
    top, low_bits = bits[0], bits[1:]

    def spread(a):
        held = [a]
        for bit in low_bits:
            held = held + [lax.ppermute(b, "mem", xor_pairs(mems, bit)) for b in held]
        return held

    masks = [0]
    for bit in low_bits:
        masks = masks + [m ^ bit for m in masks]
    masks = masks + [m ^ top for m in masks]
    near_half, far_half = [], []
    for k in range(pieces):
        band = pl.pallas_call(
            functools.partial(forecast_kernel, lats, firsts[k], counts[k], 2 if k == 0 else 0),
            out_shape=jax.ShapeDtypeStruct((counts[k], cell_count), F32),
            in_specs=[VMEM] * (7 + len(tables)),
            out_specs=VMEM,
            cost_estimate=pl.CostEstimate(flops=2000000, bytes_accessed=2000000, transcendentals=0),
            compiler_params=pltpu.CompilerParams(vmem_limit_bytes=8 << 20),
        )(ensemble, diffusivity, north_wind, near[k], far[k], near[0], far[0], *tables)
        far_half.append(lax.ppermute(band, "mem", xor_pairs(mems, top)))
        near_half.append(spread(band))

    def add_moments(stage, before, count):
        members = sum(a.shape[0] for a in stage)
        *after, stage_seen = pl.pallas_call(
            functools.partial(moment_kernel, len(before) > 0, count + members, longitudes),
            out_shape=[
                jax.ShapeDtypeStruct((observations, observations), F32),
                jax.ShapeDtypeStruct((observations, own_cells), F32),
                jax.ShapeDtypeStruct((1, observations), F32),
                jax.ShapeDtypeStruct((1, own_cells), F32),
                jax.ShapeDtypeStruct((members, observations), F32),
            ],
            in_specs=[SMEM] + [VMEM] * (1 + len(before) + len(stage)),
            out_specs=[VMEM] * 5,
            cost_estimate=pl.CostEstimate(flops=800000000, bytes_accessed=3000000, transcendentals=0),
            compiler_params=pltpu.CompilerParams(vmem_limit_bytes=16 << 20),
        )(*tables[:2], *before, *stage)
        return after, stage_seen

    stage = [near_half[k][j] for k in range(pieces) for j in range(mems // 2)]
    flat, order = stage, [(j, firsts[k]) for k in range(pieces) for j in range(mems // 2)]
    before, stage_seen = add_moments(stage, (), 0)
    seen = [stage_seen]
    for k in range(pieces):
        stage = spread(far_half[k])
        if k < pieces - 1:
            before, stage_seen = add_moments(stage, before, sum(a.shape[0] for a in flat))
            seen.append(stage_seen)
        flat = flat + stage
        order = order + [(j, firsts[k]) for j in range(mems // 2, mems)]
    outs = pl.pallas_call(
        functools.partial(
            gain_kernel, len(seen), len(stage), order, longitudes
        ),
        out_shape=[jax.ShapeDtypeStruct((local, own_cells), F32) for _ in masks],
        in_specs=[SMEM] + [VMEM] * (3 + len(before) + len(seen) + len(flat)),
        out_specs=[VMEM] * mems,
        scratch_shapes=[pltpu.VMEM((observations, observations), F32)],
        cost_estimate=pl.CostEstimate(flops=5000000000, bytes_accessed=4000000, transcendentals=0),
        compiler_params=pltpu.CompilerParams(vmem_limit_bytes=24 << 20),
        name="gain",
    )(*tables, *before, *seen, *flat)
    came = {0: outs[0]}
    for mask in sorted(masks[1:], reverse=True):
        pairs = [(i, i ^ mask) for i in range(mems)]
        came[mask] = lax.ppermute(outs[masks.index(mask)], "mem", pairs)
    return pl.pallas_call(
        functools.partial(place_kernel, masks, longitudes),
        out_shape=jax.ShapeDtypeStruct((local, rows, longitudes), F32),
        in_specs=[VMEM] * mems,
        out_specs=VMEM,
        cost_estimate=pl.CostEstimate(flops=100000, bytes_accessed=600000, transcendentals=0),
        compiler_params=pltpu.CompilerParams(vmem_limit_bytes=8 << 20),
        name="place",
    )(*[came[m] for m in masks])


def solution(mesh):
    return jax.shard_map(
        body,
        mesh=mesh,
        in_specs=(
            P("mem", "lat", None),
            P("lat", None),
            P("lat", None),
            P("lat", None, None),
            P("lat", None, None),
            P("lat", "mem", None),
            P("lat", "mem", None),
        ),
        out_specs=P("mem", "lat", None),
        check_vma=False,
    )
```

```python
import functools

import jax
import jax.numpy as jnp
from jax import lax
from jax.experimental import pallas as pl
from jax.experimental.pallas import tpu as pltpu
from jax.sharding import PartitionSpec as P


ADVECTION = 0.1
F32 = jnp.float32
BF16 = jnp.bfloat16
VMEM = pl.BlockSpec(memory_space=pltpu.VMEM)
SMEM = pl.BlockSpec(memory_space=pltpu.SMEM)


def xor_pairs(count, bit):
    return [(i, i ^ bit) for i in range(count)]


def piece_counts(local):
    unit = 8 if local % 8 == 0 else 1
    whole = local // unit
    first = (whole + 1) // 2
    return [n * unit for n in (first, whole - first) if n]


def step(rows, diffusivity, north_wind):
    out = []
    for r in range(1, len(rows) - 1):
        north, centre, south = rows[r - 1], rows[r], rows[r + 1]
        last = centre.shape[1] - 1
        eastern = pltpu.roll(centre, last, 1)
        western = pltpu.roll(centre, 1, 1)
        out.append(
            centre
            - ADVECTION * centre * (eastern - western)
            - north_wind[r - 1] * (south - north)
            + diffusivity[r - 1] * (eastern + western + north + south - 4.0 * centre)
        )
    return out


def forecast_kernel(lats, first, count, lead, own, dif, wind, near, far, coef_near, coef_far, *tables_and_out):
    out = tables_and_out[-1]
    place = lax.axis_index("lat")
    even = lax.rem(place, 2) == 0
    inner = (place > 0) & (place < lats - 1)
    rows, longitudes = own.shape[1], own.shape[2]
    edge = near.shape[1]

    def pick(a, b):
        return jnp.where(even, a, b)

    def members(ref, r):
        return ref[lead : lead + count, r, :]

    def beyond(x):
        return jnp.where(inner, x, 0.0)

    low = [pick(beyond(members(far, r)), members(near, r)) for r in (edge - 2, edge - 1)]
    high = [pick(members(near, r), beyond(members(far, r))) for r in (0, 1)]
    here = [own[first : first + count, r, :] for r in range(rows)]

    def coefficient(which, ref):
        before = pick(beyond(coef_far[which : which + 1, edge - 1, :]), coef_near[which : which + 1, edge - 1, :])
        after = pick(coef_near[which : which + 1, 0, :], beyond(coef_far[which : which + 1, 0, :]))
        return [before] + [ref[r : r + 1, :] for r in range(rows)] + [after]

    d, w = coefficient(0, dif), coefficient(1, wind)
    once = step(low + here + high, d, w)
    twice = step(once, d[1:-1], w[1:-1])
    for r in range(rows):
        out[:, r * longitudes : (r + 1) * longitudes] = twice[r]


def split(x):
    high = x.astype(BF16)
    return high, (x - high.astype(F32)).astype(BF16)


def dot3(a, b, width=256):
    rows = a[0].shape[0]
    mul = functools.partial(jnp.dot, preferred_element_type=F32)
    stacked = jnp.concatenate(a, axis=0)
    out = []
    for at in range(0, b[0].shape[1], width):
        both = mul(stacked, b[0][:, at : at + width])
        out.append(both[:rows] + (both[rows:] + mul(a[0], b[1][:, at : at + width])))
    return jnp.concatenate(out, axis=1)


def dot1(a, b, width=256):
    mul = functools.partial(jnp.dot, preferred_element_type=F32)
    return jnp.concatenate([mul(a, b[:, at : at + width]) for at in range(0, b.shape[1], width)], axis=1)


def observe(parts, longitudes, own_cells, blocks, flags):
    patch = lax.axis_index("mem")
    block_count = blocks.shape[1]
    width = flags.shape[1] // block_count
    row_blocks = longitudes // width
    flag = flags[pl.ds(patch, 1), :]
    lane = lax.broadcasted_iota(jnp.int32, (1, width), 1)
    columns = []
    for i in range(block_count):
        c = blocks[patch, i]
        row = lax.div(c, row_blocks)
        n = row * row_blocks + lax.rem(c - row * row_blocks + 1, row_blocks)
        averaged = flag[:, i * width : (i + 1) * width] == 1
        values = []
        for part in parts:
            direct = part[:, pl.ds(pl.multiple_of(c * width, width), width)]
            beyond = part[:, pl.ds(pl.multiple_of(n * width, width), width)]
            east = pltpu.roll(jnp.where(lane == 0, beyond, direct), width - 1, 1)
            values.append(jnp.where(averaged, 0.5 * (direct + east), direct))
        columns.append(jnp.concatenate(values, axis=0))
    return jnp.concatenate(columns, axis=1), own(parts, own_cells)


def own(parts, own_cells):
    at = pl.multiple_of(lax.axis_index("mem") * own_cells, own_cells)
    return jnp.concatenate([part[:, pl.ds(at, own_cells)] for part in parts], axis=0)


def doubled(x):
    high, low = split(x)
    return jnp.concatenate([high, high, low, low], axis=0)


def moments(seen, cells, before, count):
    if before is None:
        seen_mean = jnp.sum(seen, axis=0, keepdims=True) * (1.0 / count)
        cell_mean = jnp.sum(cells, axis=0, keepdims=True) * (1.0 / count)
        left = seen - seen_mean
        right, right_cells = left, cells - cell_mean
    else:
        left, right_cells = seen - before[0], cells - before[1]
        shift = jnp.sum(left, axis=0, keepdims=True) * (1.0 / count)
        cell_shift = jnp.sum(right_cells, axis=0, keepdims=True) * (1.0 / count)
        seen_mean, cell_mean = before[0] + shift, before[1] + cell_shift
        right, right_cells = left - shift, right_cells - cell_shift
    turned = jnp.concatenate(split(left), axis=0).T
    turned = jnp.concatenate([turned, turned], axis=1)
    return dot1(turned, doubled(right)), dot1(turned, doubled(right_cells)), seen_mean, cell_mean


def moment_kernel(has_before, count, longitudes, blocks, flags, *refs):
    refs = list(refs)
    outs = refs[-5:]
    before = refs[:4] if has_before else None
    parts = refs[4 if has_before else 0 : -5]
    seen, cells = observe(parts, longitudes, outs[1].shape[1], blocks, flags)
    means = None if before is None else (before[2][...], before[3][...])
    square, cross, seen_mean, cell_mean = moments(seen, cells, means, count)
    if before is not None:
        square, cross = square + before[0][...], cross + before[1][...]
    for out, value in zip(outs, (square, cross, seen_mean, cell_mean, seen)):
        out[...] = value


def square(x):
    half = x[0].shape[0] // 2
    first, second = slice(0, half), slice(half, 2 * half)

    def block(rows, columns):
        mul = functools.partial(jnp.dot, preferred_element_type=F32)
        (high, low), (high_right, low_right) = [p[rows] for p in x], [p[:, columns] for p in x]
        quarter = half // 2
        out = []
        for at in (0, quarter):
            h, l = high[at : at + quarter], low[at : at + quarter]
            both = mul(jnp.concatenate([h, l], axis=0), high_right)
            out.append(both[:quarter] + (both[quarter:] + mul(h, low_right)))
        return jnp.concatenate(out, axis=0)

    corner = block(first, second)
    above = jnp.concatenate([block(first, first), corner], axis=1)
    below = jnp.concatenate([corner.T, block(second, second)], axis=1)
    return jnp.concatenate([above, below], axis=0)


def gain_kernel(earlier, last, near_parts, order, longitudes, blocks, flags, values, errors, *refs):
    cov, left = refs[-1], refs[-10:-1]
    outs = refs[4 + earlier + len(order) : -10]
    before, first_seen, parts = refs[:4], refs[4 : 4 + earlier], refs[4 + earlier : 4 + earlier + len(order)]
    own_cells = outs[0].shape[1]
    near_rows = left[0].shape[0]
    total = sum(part.shape[0] for part in parts)
    last_seen, last_cells = observe(parts[-last:], longitudes, own_cells, blocks, flags)
    square_sum, cross, seen_mean, _ = moments(last_seen, last_cells, (before[2][...], before[3][...]), total)
    cov[...] = square_sum + before[0][...]
    tile = 128
    down = lax.broadcasted_iota(jnp.int32, (tile, tile), 0)
    across = lax.broadcasted_iota(jnp.int32, (tile, tile), 1)
    for at in range(0, cov.shape[0], tile):
        here = slice(at, at + tile)
        cov[here, here] += jnp.where(down == across, errors[:, here] * (total - 1.0), 0.0)
    covariance = cov[...]
    size = jnp.abs(covariance)
    root = lax.rsqrt(jnp.sum(size, axis=0, keepdims=True))
    root_down = lax.rsqrt(jnp.sum(size, axis=1, keepdims=True))
    cross = split((cross + before[1][...]) * root_down)
    seen = jnp.concatenate([ref[...] for ref in first_seen] + [last_seen], axis=0)
    start = ((values[...] - seen_mean) - 0.5 * (seen - seen_mean)) * root
    b1 = (covariance * root_down) * root
    s1 = split(b1)
    b2 = 2.0 * b1 - square(s1)
    s2 = split(b2)
    b4 = 2.0 * b2 - square(s2)
    s4 = split(b4)
    for out, value in zip(left, (start[:near_rows],) + s4 + s2 + s1 + cross):
        out[...] = value
    finish(start[near_rows:], s4, (s2, s1), cross, parts[near_parts:], order[near_parts:], outs)


def finish(start, s4, factors, cross, parts, order, outs):
    q = start + (start - dot1(start.astype(BF16), s4[0]))
    for _ in range(2):
        q = start + (q - dot3(split(q), s4))
    for factor in factors:
        q = 2.0 * q - dot3(split(q), factor)
    update = dot3(split(q), cross)
    at = 0
    for part, (j, row) in zip(parts, order):
        size = part.shape[0]
        outs[j][row : row + size, :] = own([part], outs[j].shape[1]) + update[at : at + size, :]
        at += size


def finish_kernel(order, start, *refs):
    s4, s2, s1, cross = [(refs[i][...], refs[i + 1][...]) for i in (0, 2, 4, 6)]
    parts, outs = refs[8 : 8 + len(order)], refs[8 + len(order) :]
    finish(start[...], s4, (s2, s1), cross, parts, order, outs)


def place_kernel(masks, longitudes, *refs):
    sources, out = refs[:-1], refs[-1]
    here = lax.axis_index("mem")
    width = sources[0].shape[1]
    found = [source[...] for source in sources]
    for patch in range(len(masks)):
        value = found[0]
        for m, candidate in zip(masks[1:], found[1:]):
            value = jnp.where((here ^ m) == patch, candidate, value)
        row, column = divmod(patch * width, longitudes)
        out[:, row, column : column + width] = value


def body(
    ensemble,
    diffusivity,
    north_wind,
    observed_blocks,
    eastern_average_flags,
    observed_values,
    observed_error,
):
    local, rows, longitudes = ensemble.shape
    lats, mems = lax.axis_size("lat"), lax.axis_size("mem")
    observations = observed_values.shape[-1]
    cell_count = rows * longitudes
    own_cells = cell_count // mems
    near_pairs = xor_pairs(lats, 1)
    far_pairs = [(i, i + 2) for i in range(0, lats - 2, 2)] + [(i, i - 2) for i in range(3, lats, 2)]
    far_pairs += [(lats - 2, lats - 1), (1, 0)]

    def edges(block):
        if block.shape[1] == 2:
            return block
        return jnp.concatenate([block[:, :2], block[:, -2:]], axis=1)

    counts = piece_counts(local)
    pieces = len(counts)
    firsts = [sum(counts[:k]) for k in range(pieces)]
    bits = [1 << k for k in reversed(range(mems.bit_length() - 1))]
    coefficients = edges(jnp.stack([diffusivity, north_wind]))
    near, far = [], []
    for k in range(pieces):
        own = edges(ensemble[firsts[k] : firsts[k] + counts[k]])
        if k == 0:
            own = jnp.concatenate([coefficients, own], axis=0)
        near.append(lax.ppermute(own, "lat", near_pairs))
    for k in range(pieces):
        far.append(lax.ppermute(near[k], "lat", far_pairs))
    tables = observed_blocks[0], eastern_average_flags[0], observed_values[0], observed_error[0]
    top, low_bits = bits[0], bits[1:]

    def spread(a):
        held = [a]
        for bit in low_bits:
            held = held + [lax.ppermute(b, "mem", xor_pairs(mems, bit)) for b in held]
        return held

    masks = [0]
    for bit in low_bits:
        masks = masks + [m ^ bit for m in masks]
    masks = masks + [m ^ top for m in masks]
    near_half, far_half = [], []
    for k in range(pieces):
        band = pl.pallas_call(
            functools.partial(forecast_kernel, lats, firsts[k], counts[k], 2 if k == 0 else 0),
            out_shape=jax.ShapeDtypeStruct((counts[k], cell_count), F32),
            in_specs=[VMEM] * (7 + len(tables)),
            out_specs=VMEM,
            cost_estimate=pl.CostEstimate(flops=2000000, bytes_accessed=2000000, transcendentals=0),
            compiler_params=pltpu.CompilerParams(vmem_limit_bytes=8 << 20),
        )(ensemble, diffusivity, north_wind, near[k], far[k], near[0], far[0], *tables)
        far_half.append(lax.ppermute(band, "mem", xor_pairs(mems, top)))
        near_half.append(spread(band))

    def add_moments(stage, before, count):
        members = sum(a.shape[0] for a in stage)
        *after, stage_seen = pl.pallas_call(
            functools.partial(moment_kernel, len(before) > 0, count + members, longitudes),
            out_shape=[
                jax.ShapeDtypeStruct((observations, observations), F32),
                jax.ShapeDtypeStruct((observations, own_cells), F32),
                jax.ShapeDtypeStruct((1, observations), F32),
                jax.ShapeDtypeStruct((1, own_cells), F32),
                jax.ShapeDtypeStruct((members, observations), F32),
            ],
            in_specs=[SMEM] + [VMEM] * (1 + len(before) + len(stage)),
            out_specs=[VMEM] * 5,
            cost_estimate=pl.CostEstimate(flops=800000000, bytes_accessed=3000000, transcendentals=0),
            compiler_params=pltpu.CompilerParams(vmem_limit_bytes=16 << 20),
        )(*tables[:2], *before, *stage)
        return after, stage_seen

    stage = [near_half[k][j] for k in range(pieces) for j in range(mems // 2)]
    flat, order = stage, [(j, firsts[k]) for k in range(pieces) for j in range(mems // 2)]
    before, stage_seen = add_moments(stage, (), 0)
    seen = [stage_seen]
    for k in range(pieces):
        stage = spread(far_half[k])
        if k < pieces - 1:
            before, stage_seen = add_moments(stage, before, sum(a.shape[0] for a in flat))
            seen.append(stage_seen)
        flat = flat + stage
        order = order + [(j, firsts[k]) for j in range(mems // 2, mems)]
    near_parts = pieces * (mems // 2)
    near_order, far_order = order[:near_parts], [(j - mems // 2, row) for j, row in order[near_parts:]]
    to_member = jax.ShapeDtypeStruct((local, own_cells), F32)
    far_mems = mems - mems // 2
    part_of_product = [jax.ShapeDtypeStruct((observations, observations), BF16)] * 2
    part_of_cross = [jax.ShapeDtypeStruct((observations, own_cells), BF16)] * 2
    near_rows = local * (mems // 2)
    done = pl.pallas_call(
        functools.partial(
            gain_kernel, len(seen), len(stage), near_parts, near_order + far_order, longitudes
        ),
        out_shape=[to_member] * far_mems
        + [jax.ShapeDtypeStruct((near_rows, observations), F32)]
        + part_of_product * 3
        + part_of_cross,
        in_specs=[SMEM] + [VMEM] * (3 + len(before) + len(seen) + len(flat)),
        out_specs=[VMEM] * (far_mems + 9),
        scratch_shapes=[pltpu.VMEM((observations, observations), F32)],
        cost_estimate=pl.CostEstimate(flops=5000000000, bytes_accessed=4000000, transcendentals=0),
        compiler_params=pltpu.CompilerParams(vmem_limit_bytes=24 << 20),
        name="gain",
    )(*tables, *before, *seen, *flat)
    far_outs = done[:far_mems]
    near_outs = pl.pallas_call(
        functools.partial(finish_kernel, near_order),
        out_shape=[to_member] * (mems // 2),
        in_specs=[VMEM] * (9 + near_parts),
        out_specs=[VMEM] * (mems // 2),
        cost_estimate=pl.CostEstimate(flops=600000000, bytes_accessed=2000000, transcendentals=0),
        compiler_params=pltpu.CompilerParams(vmem_limit_bytes=16 << 20),
        name="finish",
    )(*done[far_mems:], *flat[:near_parts])
    outs = list(near_outs) + list(far_outs)
    came = {0: outs[0]}
    for mask in sorted(masks[1:], reverse=True):
        pairs = [(i, i ^ mask) for i in range(mems)]
        came[mask] = lax.ppermute(outs[masks.index(mask)], "mem", pairs)
    return pl.pallas_call(
        functools.partial(place_kernel, masks, longitudes),
        out_shape=jax.ShapeDtypeStruct((local, rows, longitudes), F32),
        in_specs=[VMEM] * mems,
        out_specs=VMEM,
        cost_estimate=pl.CostEstimate(flops=100000, bytes_accessed=600000, transcendentals=0),
        compiler_params=pltpu.CompilerParams(vmem_limit_bytes=8 << 20),
        name="place",
    )(*[came[m] for m in masks])


def solution(mesh):
    return jax.shard_map(
        body,
        mesh=mesh,
        in_specs=(
            P("mem", "lat", None),
            P("lat", None),
            P("lat", None),
            P("lat", None, None),
            P("lat", None, None),
            P("lat", "mem", None),
            P("lat", "mem", None),
        ),
        out_specs=P("mem", "lat", None),
        check_vma=False,
    )
```

```python
import functools

import jax
import jax.numpy as jnp
from jax import lax
from jax.experimental import pallas as pl
from jax.experimental.pallas import tpu as pltpu
from jax.sharding import PartitionSpec as P


ADVECTION = 0.1
F32 = jnp.float32
BF16 = jnp.bfloat16
VMEM = pl.BlockSpec(memory_space=pltpu.VMEM)
SMEM = pl.BlockSpec(memory_space=pltpu.SMEM)


def xor_pairs(count, bit):
    return [(i, i ^ bit) for i in range(count)]


def piece_counts(local):
    unit = 8 if local % 8 == 0 else 1
    whole = local // unit
    first = (whole + 1) // 2
    return [n * unit for n in (first, whole - first) if n]


def step(rows, diffusivity, north_wind):
    out = []
    for r in range(1, len(rows) - 1):
        north, centre, south = rows[r - 1], rows[r], rows[r + 1]
        last = centre.shape[1] - 1
        eastern = pltpu.roll(centre, last, 1)
        western = pltpu.roll(centre, 1, 1)
        out.append(
            centre
            - ADVECTION * centre * (eastern - western)
            - north_wind[r - 1] * (south - north)
            + diffusivity[r - 1] * (eastern + western + north + south - 4.0 * centre)
        )
    return out


def forecast_kernel(lats, first, count, lead, own, dif, wind, near, far, coef_near, coef_far, *tables_and_out):
    out = tables_and_out[-1]
    place = lax.axis_index("lat")
    even = lax.rem(place, 2) == 0
    inner = (place > 0) & (place < lats - 1)
    rows, longitudes = own.shape[1], own.shape[2]
    edge = near.shape[1]

    def pick(a, b):
        return jnp.where(even, a, b)

    def members(ref, r):
        return ref[lead : lead + count, r, :]

    def beyond(x):
        return jnp.where(inner, x, 0.0)

    low = [pick(beyond(members(far, r)), members(near, r)) for r in (edge - 2, edge - 1)]
    high = [pick(members(near, r), beyond(members(far, r))) for r in (0, 1)]
    here = [own[first : first + count, r, :] for r in range(rows)]

    def coefficient(which, ref):
        before = pick(beyond(coef_far[which : which + 1, edge - 1, :]), coef_near[which : which + 1, edge - 1, :])
        after = pick(coef_near[which : which + 1, 0, :], beyond(coef_far[which : which + 1, 0, :]))
        return [before] + [ref[r : r + 1, :] for r in range(rows)] + [after]

    d, w = coefficient(0, dif), coefficient(1, wind)
    once = step(low + here + high, d, w)
    twice = step(once, d[1:-1], w[1:-1])
    for r in range(rows):
        out[:, r * longitudes : (r + 1) * longitudes] = twice[r]


def split(x):
    high = x.astype(BF16)
    return high, (x - high.astype(F32)).astype(BF16)


def dot3(a, b, width=256):
    rows = a[0].shape[0]
    mul = functools.partial(jnp.dot, preferred_element_type=F32)
    stacked = jnp.concatenate(a, axis=0)
    out = []
    for at in range(0, b[0].shape[1], width):
        both = mul(stacked, b[0][:, at : at + width])
        out.append(both[:rows] + (both[rows:] + mul(a[0], b[1][:, at : at + width])))
    return jnp.concatenate(out, axis=1)


def dot1(a, b, width=256):
    mul = functools.partial(jnp.dot, preferred_element_type=F32)
    return jnp.concatenate([mul(a, b[:, at : at + width]) for at in range(0, b.shape[1], width)], axis=1)


def observe(parts, longitudes, own_cells, blocks, flags):
    patch = lax.axis_index("mem")
    block_count = blocks.shape[1]
    width = flags.shape[1] // block_count
    row_blocks = longitudes // width
    flag = flags[pl.ds(patch, 1), :]
    lane = lax.broadcasted_iota(jnp.int32, (1, width), 1)
    columns = []
    for i in range(block_count):
        c = blocks[patch, i]
        row = lax.div(c, row_blocks)
        n = row * row_blocks + lax.rem(c - row * row_blocks + 1, row_blocks)
        averaged = flag[:, i * width : (i + 1) * width] == 1
        values = []
        for part in parts:
            direct = part[:, pl.ds(pl.multiple_of(c * width, width), width)]
            beyond = part[:, pl.ds(pl.multiple_of(n * width, width), width)]
            east = pltpu.roll(jnp.where(lane == 0, beyond, direct), width - 1, 1)
            values.append(jnp.where(averaged, 0.5 * (direct + east), direct))
        columns.append(jnp.concatenate(values, axis=0))
    return jnp.concatenate(columns, axis=1), own(parts, own_cells)


def own(parts, own_cells):
    at = pl.multiple_of(lax.axis_index("mem") * own_cells, own_cells)
    return jnp.concatenate([part[:, pl.ds(at, own_cells)] for part in parts], axis=0)


def doubled(x):
    high, low = split(x)
    return jnp.concatenate([high, high, low, low], axis=0)


def moments(seen, cells, before, count):
    if before is None:
        seen_mean = jnp.sum(seen, axis=0, keepdims=True) * (1.0 / count)
        cell_mean = jnp.sum(cells, axis=0, keepdims=True) * (1.0 / count)
        left = seen - seen_mean
        right, right_cells = left, cells - cell_mean
    else:
        left, right_cells = seen - before[0], cells - before[1]
        shift = jnp.sum(left, axis=0, keepdims=True) * (1.0 / count)
        cell_shift = jnp.sum(right_cells, axis=0, keepdims=True) * (1.0 / count)
        seen_mean, cell_mean = before[0] + shift, before[1] + cell_shift
        right, right_cells = left - shift, right_cells - cell_shift
    turned = jnp.concatenate(split(left), axis=0).T
    turned = jnp.concatenate([turned, turned], axis=1)
    return dot1(turned, doubled(right)), dot1(turned, doubled(right_cells)), seen_mean, cell_mean


def moment_kernel(has_before, count, longitudes, blocks, flags, *refs):
    refs = list(refs)
    outs = refs[-5:]
    before = refs[:4] if has_before else None
    parts = refs[4 if has_before else 0 : -5]
    seen, cells = observe(parts, longitudes, outs[1].shape[1], blocks, flags)
    means = None if before is None else (before[2][...], before[3][...])
    square, cross, seen_mean, cell_mean = moments(seen, cells, means, count)
    if before is not None:
        square, cross = square + before[0][...], cross + before[1][...]
    for out, value in zip(outs, (square, cross, seen_mean, cell_mean, seen)):
        out[...] = value


def square(x):
    half = x[0].shape[0] // 2
    first, second = slice(0, half), slice(half, 2 * half)

    def block(rows, columns):
        mul = functools.partial(jnp.dot, preferred_element_type=F32)
        (high, low), (high_right, low_right) = [p[rows] for p in x], [p[:, columns] for p in x]
        quarter = half // 2
        out = []
        for at in (0, quarter):
            h, l = high[at : at + quarter], low[at : at + quarter]
            both = mul(jnp.concatenate([h, l], axis=0), high_right)
            out.append(both[:quarter] + (both[quarter:] + mul(h, low_right)))
        return jnp.concatenate(out, axis=0)

    corner = block(first, second)
    above = jnp.concatenate([block(first, first), corner], axis=1)
    below = jnp.concatenate([corner.T, block(second, second)], axis=1)
    return jnp.concatenate([above, below], axis=0)


def gain_kernel(earlier, last, near_parts, order, longitudes, blocks, flags, values, errors, *refs):
    cov, left = refs[-1], refs[-11:-1]
    outs = refs[4 + earlier + len(order) : -11]
    before, first_seen, parts = refs[:4], refs[4 : 4 + earlier], refs[4 + earlier : 4 + earlier + len(order)]
    own_cells = outs[0].shape[1]
    total = sum(part.shape[0] for part in parts)
    last_seen, last_cells = observe(parts[-last:], longitudes, own_cells, blocks, flags)
    square_sum, cross, seen_mean, _ = moments(last_seen, last_cells, (before[2][...], before[3][...]), total)
    cov[...] = square_sum + before[0][...]
    tile = 128
    down = lax.broadcasted_iota(jnp.int32, (tile, tile), 0)
    across = lax.broadcasted_iota(jnp.int32, (tile, tile), 1)
    for at in range(0, cov.shape[0], tile):
        here = slice(at, at + tile)
        cov[here, here] += jnp.where(down == across, errors[:, here] * (total - 1.0), 0.0)
    covariance = cov[...]
    size = jnp.abs(covariance)
    root = lax.rsqrt(jnp.sum(size, axis=0, keepdims=True))
    root_down = lax.rsqrt(jnp.sum(size, axis=1, keepdims=True))
    cross = split((cross + before[1][...]) * root_down)
    seen = jnp.concatenate([ref[...] for ref in first_seen[1:]] + [last_seen], axis=0)
    start = weights(seen, seen_mean, values, root)
    b1 = (covariance * root_down) * root
    s1 = split(b1)
    b2 = 2.0 * b1 - square(s1)
    s2 = split(b2)
    b4 = 2.0 * b2 - square(s2)
    s4 = split(b4)
    for out, value in zip(left, (seen_mean, root) + s4 + s2 + s1 + cross):
        out[...] = value
    finish(start, s4, (s2, s1), cross, parts[near_parts:], order[near_parts:], outs)


def weights(seen, seen_mean, values, root):
    return ((values[...] - seen_mean) - 0.5 * (seen - seen_mean)) * root


def finish(start, s4, factors, cross, parts, order, outs):
    q = start + (start - dot1(start.astype(BF16), s4[0]))
    for _ in range(2):
        q = start + (q - dot3(split(q), s4))
    for factor in factors:
        q = 2.0 * q - dot3(split(q), factor)
    update = dot3(split(q), cross)
    at = 0
    for part, (j, row) in zip(parts, order):
        size = part.shape[0]
        outs[j][row : row + size, :] = own([part], outs[j].shape[1]) + update[at : at + size, :]
        at += size


def finish_kernel(order, seen, values, seen_mean, root, *refs):
    s4, s2, s1, cross = [(refs[i][...], refs[i + 1][...]) for i in (0, 2, 4, 6)]
    parts, outs = refs[8 : 8 + len(order)], refs[8 + len(order) :]
    start = weights(seen[...], seen_mean[...], values, root[...])
    finish(start, s4, (s2, s1), cross, parts, order, outs)


def place_kernel(masks, longitudes, *refs):
    sources, out = refs[:-1], refs[-1]
    here = lax.axis_index("mem")
    width = sources[0].shape[1]
    found = [source[...] for source in sources]
    for patch in range(len(masks)):
        value = found[0]
        for m, candidate in zip(masks[1:], found[1:]):
            value = jnp.where((here ^ m) == patch, candidate, value)
        row, column = divmod(patch * width, longitudes)
        out[:, row, column : column + width] = value


def body(
    ensemble,
    diffusivity,
    north_wind,
    observed_blocks,
    eastern_average_flags,
    observed_values,
    observed_error,
):
    local, rows, longitudes = ensemble.shape
    lats, mems = lax.axis_size("lat"), lax.axis_size("mem")
    observations = observed_values.shape[-1]
    cell_count = rows * longitudes
    own_cells = cell_count // mems
    near_pairs = xor_pairs(lats, 1)
    far_pairs = [(i, i + 2) for i in range(0, lats - 2, 2)] + [(i, i - 2) for i in range(3, lats, 2)]
    far_pairs += [(lats - 2, lats - 1), (1, 0)]

    def edges(block):
        if block.shape[1] == 2:
            return block
        return jnp.concatenate([block[:, :2], block[:, -2:]], axis=1)

    counts = piece_counts(local)
    pieces = len(counts)
    firsts = [sum(counts[:k]) for k in range(pieces)]
    bits = [1 << k for k in reversed(range(mems.bit_length() - 1))]
    coefficients = edges(jnp.stack([diffusivity, north_wind]))
    near, far = [], []
    for k in range(pieces):
        own = edges(ensemble[firsts[k] : firsts[k] + counts[k]])
        if k == 0:
            own = jnp.concatenate([coefficients, own], axis=0)
        near.append(lax.ppermute(own, "lat", near_pairs))
    for k in range(pieces):
        far.append(lax.ppermute(near[k], "lat", far_pairs))
    tables = observed_blocks[0], eastern_average_flags[0], observed_values[0], observed_error[0]
    top, low_bits = bits[0], bits[1:]

    def spread(a):
        held = [a]
        for bit in low_bits:
            held = held + [lax.ppermute(b, "mem", xor_pairs(mems, bit)) for b in held]
        return held

    masks = [0]
    for bit in low_bits:
        masks = masks + [m ^ bit for m in masks]
    masks = masks + [m ^ top for m in masks]
    near_half, far_half = [], []
    for k in range(pieces):
        band = pl.pallas_call(
            functools.partial(forecast_kernel, lats, firsts[k], counts[k], 2 if k == 0 else 0),
            out_shape=jax.ShapeDtypeStruct((counts[k], cell_count), F32),
            in_specs=[VMEM] * (7 + len(tables)),
            out_specs=VMEM,
            cost_estimate=pl.CostEstimate(flops=2000000, bytes_accessed=2000000, transcendentals=0),
            compiler_params=pltpu.CompilerParams(vmem_limit_bytes=8 << 20),
        )(ensemble, diffusivity, north_wind, near[k], far[k], near[0], far[0], *tables)
        far_half.append(lax.ppermute(band, "mem", xor_pairs(mems, top)))
        near_half.append(spread(band))

    def add_moments(stage, before, count):
        members = sum(a.shape[0] for a in stage)
        *after, stage_seen = pl.pallas_call(
            functools.partial(moment_kernel, len(before) > 0, count + members, longitudes),
            out_shape=[
                jax.ShapeDtypeStruct((observations, observations), F32),
                jax.ShapeDtypeStruct((observations, own_cells), F32),
                jax.ShapeDtypeStruct((1, observations), F32),
                jax.ShapeDtypeStruct((1, own_cells), F32),
                jax.ShapeDtypeStruct((members, observations), F32),
            ],
            in_specs=[SMEM] + [VMEM] * (1 + len(before) + len(stage)),
            out_specs=[VMEM] * 5,
            cost_estimate=pl.CostEstimate(flops=800000000, bytes_accessed=3000000, transcendentals=0),
            compiler_params=pltpu.CompilerParams(vmem_limit_bytes=16 << 20),
        )(*tables[:2], *before, *stage)
        return after, stage_seen

    stage = [near_half[k][j] for k in range(pieces) for j in range(mems // 2)]
    flat, order = stage, [(j, firsts[k]) for k in range(pieces) for j in range(mems // 2)]
    before, stage_seen = add_moments(stage, (), 0)
    seen = [stage_seen]
    for k in range(pieces):
        stage = spread(far_half[k])
        if k < pieces - 1:
            before, stage_seen = add_moments(stage, before, sum(a.shape[0] for a in flat))
            seen.append(stage_seen)
        flat = flat + stage
        order = order + [(j, firsts[k]) for j in range(mems // 2, mems)]
    near_parts = pieces * (mems // 2)
    near_order, far_order = order[:near_parts], [(j - mems // 2, row) for j, row in order[near_parts:]]
    to_member = jax.ShapeDtypeStruct((local, own_cells), F32)
    far_mems = mems - mems // 2
    part_of_product = [jax.ShapeDtypeStruct((observations, observations), BF16)] * 2
    part_of_cross = [jax.ShapeDtypeStruct((observations, own_cells), BF16)] * 2
    done = pl.pallas_call(
        functools.partial(
            gain_kernel, len(seen), len(stage), near_parts, near_order + far_order, longitudes
        ),
        out_shape=[to_member] * far_mems
        + [jax.ShapeDtypeStruct((1, observations), F32)] * 2
        + part_of_product * 3
        + part_of_cross,
        in_specs=[SMEM] + [VMEM] * (3 + len(before) + len(seen) + len(flat)),
        out_specs=[VMEM] * (far_mems + 10),
        scratch_shapes=[pltpu.VMEM((observations, observations), F32)],
        cost_estimate=pl.CostEstimate(flops=5000000000, bytes_accessed=4000000, transcendentals=0),
        compiler_params=pltpu.CompilerParams(vmem_limit_bytes=24 << 20),
        name="gain",
    )(*tables, *before, *seen, *flat)
    far_outs = done[:far_mems]
    near_outs = pl.pallas_call(
        functools.partial(finish_kernel, near_order),
        out_shape=[to_member] * (mems // 2),
        in_specs=[VMEM] * (12 + near_parts),
        out_specs=[VMEM] * (mems // 2),
        cost_estimate=pl.CostEstimate(flops=600000000, bytes_accessed=2000000, transcendentals=0),
        compiler_params=pltpu.CompilerParams(vmem_limit_bytes=16 << 20),
        name="finish",
    )(seen[0], observed_values[0], *done[far_mems:], *flat[:near_parts])
    outs = list(near_outs) + list(far_outs)
    came = {0: outs[0]}
    for mask in sorted(masks[1:], reverse=True):
        pairs = [(i, i ^ mask) for i in range(mems)]
        came[mask] = lax.ppermute(outs[masks.index(mask)], "mem", pairs)
    return pl.pallas_call(
        functools.partial(place_kernel, masks, longitudes),
        out_shape=jax.ShapeDtypeStruct((local, rows, longitudes), F32),
        in_specs=[VMEM] * mems,
        out_specs=VMEM,
        cost_estimate=pl.CostEstimate(flops=100000, bytes_accessed=600000, transcendentals=0),
        compiler_params=pltpu.CompilerParams(vmem_limit_bytes=8 << 20),
        name="place",
    )(*[came[m] for m in masks])


def solution(mesh):
    return jax.shard_map(
        body,
        mesh=mesh,
        in_specs=(
            P("mem", "lat", None),
            P("lat", None),
            P("lat", None),
            P("lat", None, None),
            P("lat", None, None),
            P("lat", "mem", None),
            P("lat", "mem", None),
        ),
        out_specs=P("mem", "lat", None),
        check_vma=False,
    )
```

```python
import functools

import jax
import jax.numpy as jnp
from jax import lax
from jax.experimental import pallas as pl
from jax.experimental.pallas import tpu as pltpu
from jax.sharding import PartitionSpec as P


LOTS = 2
ADVECTION = 0.1
F32 = jnp.float32
BF16 = jnp.bfloat16
VMEM = pl.BlockSpec(memory_space=pltpu.VMEM)
SMEM = pl.BlockSpec(memory_space=pltpu.SMEM)


def xor_pairs(count, bit):
    return [(i, i ^ bit) for i in range(count)]


def piece_counts(local):
    unit = 8 if local % 8 == 0 else 1
    whole = local // unit
    first = (whole + 1) // 2
    return [n * unit for n in (first, whole - first) if n]


def step(rows, diffusivity, north_wind):
    out = []
    for r in range(1, len(rows) - 1):
        north, centre, south = rows[r - 1], rows[r], rows[r + 1]
        last = centre.shape[1] - 1
        eastern = pltpu.roll(centre, last, 1)
        western = pltpu.roll(centre, 1, 1)
        out.append(
            centre
            - ADVECTION * centre * (eastern - western)
            - north_wind[r - 1] * (south - north)
            + diffusivity[r - 1] * (eastern + western + north + south - 4.0 * centre)
        )
    return out


def forecast_kernel(lats, first, count, lead, own, dif, wind, near, far, coef_near, coef_far, *tables_and_out):
    out = tables_and_out[-1]
    place = lax.axis_index("lat")
    even = lax.rem(place, 2) == 0
    inner = (place > 0) & (place < lats - 1)
    rows, longitudes = own.shape[1], own.shape[2]
    edge = near.shape[1]

    def pick(a, b):
        return jnp.where(even, a, b)

    def members(ref, r):
        return ref[lead : lead + count, r, :]

    def beyond(x):
        return jnp.where(inner, x, 0.0)

    low = [pick(beyond(members(far, r)), members(near, r)) for r in (edge - 2, edge - 1)]
    high = [pick(members(near, r), beyond(members(far, r))) for r in (0, 1)]
    here = [own[first : first + count, r, :] for r in range(rows)]

    def coefficient(which, ref):
        before = pick(beyond(coef_far[which : which + 1, edge - 1, :]), coef_near[which : which + 1, edge - 1, :])
        after = pick(coef_near[which : which + 1, 0, :], beyond(coef_far[which : which + 1, 0, :]))
        return [before] + [ref[r : r + 1, :] for r in range(rows)] + [after]

    d, w = coefficient(0, dif), coefficient(1, wind)
    once = step(low + here + high, d, w)
    twice = step(once, d[1:-1], w[1:-1])
    for r in range(rows):
        out[:, r * longitudes : (r + 1) * longitudes] = twice[r]


def split(x):
    high = x.astype(BF16)
    return high, (x - high.astype(F32)).astype(BF16)


def dot3(a, b, width=256):
    rows = a[0].shape[0]
    mul = functools.partial(jnp.dot, preferred_element_type=F32)
    stacked = jnp.concatenate(a, axis=0)
    out = []
    for at in range(0, b[0].shape[1], width):
        both = mul(stacked, b[0][:, at : at + width])
        out.append(both[:rows] + (both[rows:] + mul(a[0], b[1][:, at : at + width])))
    return jnp.concatenate(out, axis=1)


def dot1(a, b, width=256):
    mul = functools.partial(jnp.dot, preferred_element_type=F32)
    return jnp.concatenate([mul(a, b[:, at : at + width]) for at in range(0, b.shape[1], width)], axis=1)


def observe(parts, longitudes, own_cells, blocks, flags):
    patch = lax.axis_index("mem")
    block_count = blocks.shape[1]
    width = flags.shape[1] // block_count
    row_blocks = longitudes // width
    flag = flags[pl.ds(patch, 1), :]
    lane = lax.broadcasted_iota(jnp.int32, (1, width), 1)
    columns = []
    for i in range(block_count):
        c = blocks[patch, i]
        row = lax.div(c, row_blocks)
        n = row * row_blocks + lax.rem(c - row * row_blocks + 1, row_blocks)
        averaged = flag[:, i * width : (i + 1) * width] == 1
        values = []
        for part in parts:
            direct = part[:, pl.ds(pl.multiple_of(c * width, width), width)]
            beyond = part[:, pl.ds(pl.multiple_of(n * width, width), width)]
            east = pltpu.roll(jnp.where(lane == 0, beyond, direct), width - 1, 1)
            values.append(jnp.where(averaged, 0.5 * (direct + east), direct))
        columns.append(jnp.concatenate(values, axis=0))
    return jnp.concatenate(columns, axis=1), own(parts, own_cells)


def own(parts, own_cells):
    at = pl.multiple_of(lax.axis_index("mem") * own_cells, own_cells)
    return jnp.concatenate([part[:, pl.ds(at, own_cells)] for part in parts], axis=0)


def doubled(x):
    high, low = split(x)
    return jnp.concatenate([high, high, low, low], axis=0)


def moments(seen, cells, before, count):
    if before is None:
        seen_mean = jnp.sum(seen, axis=0, keepdims=True) * (1.0 / count)
        cell_mean = jnp.sum(cells, axis=0, keepdims=True) * (1.0 / count)
        left = seen - seen_mean
        right, right_cells = left, cells - cell_mean
    else:
        left, right_cells = seen - before[0], cells - before[1]
        shift = jnp.sum(left, axis=0, keepdims=True) * (1.0 / count)
        cell_shift = jnp.sum(right_cells, axis=0, keepdims=True) * (1.0 / count)
        seen_mean, cell_mean = before[0] + shift, before[1] + cell_shift
        right, right_cells = left - shift, right_cells - cell_shift
    turned = jnp.concatenate(split(left), axis=0).T
    turned = jnp.concatenate([turned, turned], axis=1)
    return dot1(turned, doubled(right)), dot1(turned, doubled(right_cells)), seen_mean, cell_mean


def moment_kernel(has_before, count, longitudes, blocks, flags, *refs):
    refs = list(refs)
    outs = refs[-5:]
    before = refs[:4] if has_before else None
    parts = refs[4 if has_before else 0 : -5]
    seen, cells = observe(parts, longitudes, outs[1].shape[1], blocks, flags)
    means = None if before is None else (before[2][...], before[3][...])
    square, cross, seen_mean, cell_mean = moments(seen, cells, means, count)
    if before is not None:
        square, cross = square + before[0][...], cross + before[1][...]
    for out, value in zip(outs, (square, cross, seen_mean, cell_mean, seen)):
        out[...] = value


def square(x):
    half = x[0].shape[0] // 2
    first, second = slice(0, half), slice(half, 2 * half)

    def block(rows, columns):
        mul = functools.partial(jnp.dot, preferred_element_type=F32)
        (high, low), (high_right, low_right) = [p[rows] for p in x], [p[:, columns] for p in x]
        quarter = half // 2
        out = []
        for at in (0, quarter):
            h, l = high[at : at + quarter], low[at : at + quarter]
            both = mul(jnp.concatenate([h, l], axis=0), high_right)
            out.append(both[:quarter] + (both[quarter:] + mul(h, low_right)))
        return jnp.concatenate(out, axis=0)

    corner = block(first, second)
    above = jnp.concatenate([block(first, first), corner], axis=1)
    below = jnp.concatenate([corner.T, block(second, second)], axis=1)
    return jnp.concatenate([above, below], axis=0)


def gain_kernel(earlier, last, near_parts, order, longitudes, blocks, flags, values, errors, *refs):
    cov, left = refs[-1], refs[-10:-1]
    outs = refs[4 + earlier + len(order) : -10]
    before, first_seen, parts = refs[:4], refs[4 : 4 + earlier], refs[4 + earlier : 4 + earlier + len(order)]
    own_cells = outs[0].shape[1]
    near_rows = left[0].shape[0]
    total = sum(part.shape[0] for part in parts)
    last_seen, last_cells = observe(parts[-last:], longitudes, own_cells, blocks, flags)
    square_sum, cross, seen_mean, _ = moments(last_seen, last_cells, (before[2][...], before[3][...]), total)
    cov[...] = square_sum + before[0][...]
    tile = 128
    down = lax.broadcasted_iota(jnp.int32, (tile, tile), 0)
    across = lax.broadcasted_iota(jnp.int32, (tile, tile), 1)
    for at in range(0, cov.shape[0], tile):
        here = slice(at, at + tile)
        cov[here, here] += jnp.where(down == across, errors[:, here] * (total - 1.0), 0.0)
    covariance = cov[...]
    size = jnp.abs(covariance)
    root = lax.rsqrt(jnp.sum(size, axis=0, keepdims=True))
    root_down = lax.rsqrt(jnp.sum(size, axis=1, keepdims=True))
    cross = split((cross + before[1][...]) * root_down)
    seen = jnp.concatenate([ref[...] for ref in first_seen] + [last_seen], axis=0)
    start = ((values[...] - seen_mean) - 0.5 * (seen - seen_mean)) * root
    b1 = (covariance * root_down) * root
    s1 = split(b1)
    b2 = 2.0 * b1 - square(s1)
    s2 = split(b2)
    b4 = 2.0 * b2 - square(s2)
    s4 = split(b4)
    for out, value in zip(left, (start[:near_rows],) + s4 + s2 + s1 + cross):
        out[...] = value
    finish(start[near_rows:], s4, (s2, s1), cross, parts[near_parts:], order[near_parts:], outs)


def finish(start, s4, factors, cross, parts, order, outs):
    q = start + (start - dot1(start.astype(BF16), s4[0]))
    for _ in range(2):
        q = start + (q - dot3(split(q), s4))
    for factor in factors:
        q = 2.0 * q - dot3(split(q), factor)
    update = dot3(split(q), cross)
    at = 0
    for part, (j, row) in zip(parts, order):
        size = part.shape[0]
        outs[j][row : row + size, :] = own([part], outs[j].shape[1]) + update[at : at + size, :]
        at += size


def finish_kernel(order, start, *refs):
    s4, s2, s1, cross = [(refs[i][...], refs[i + 1][...]) for i in (0, 2, 4, 6)]
    parts, outs = refs[8 : 8 + len(order)], refs[8 + len(order) :]
    finish(start[...], s4, (s2, s1), cross, parts, order, outs)


def place_kernel(masks, longitudes, *refs):
    sources, (out, laid, sems) = refs[:-3], refs[-3:]
    here = lax.axis_index("mem")
    lots = sems.shape[0]
    size = out.shape[0] // lots
    width = sources[0].shape[1]
    copies = []
    for lot in range(lots):
        members = slice(lot * size, (lot + 1) * size)
        found = [source[members, :] for source in sources]
        for patch in range(len(masks)):
            value = found[0]
            for m, candidate in zip(masks[1:], found[1:]):
                value = jnp.where((here ^ m) == patch, candidate, value)
            row, column = divmod(patch * width, longitudes)
            laid[members, row, column : column + width] = value
        copies.append(
            pltpu.make_async_copy(laid.at[pl.ds(lot * size, size)], out.at[pl.ds(lot * size, size)], sems.at[lot])
        )
        copies[-1].start()
    for copy in copies:
        copy.wait()


def body(
    ensemble,
    diffusivity,
    north_wind,
    observed_blocks,
    eastern_average_flags,
    observed_values,
    observed_error,
):
    local, rows, longitudes = ensemble.shape
    lats, mems = lax.axis_size("lat"), lax.axis_size("mem")
    observations = observed_values.shape[-1]
    cell_count = rows * longitudes
    own_cells = cell_count // mems
    near_pairs = xor_pairs(lats, 1)
    far_pairs = [(i, i + 2) for i in range(0, lats - 2, 2)] + [(i, i - 2) for i in range(3, lats, 2)]
    far_pairs += [(lats - 2, lats - 1), (1, 0)]

    def edges(block):
        if block.shape[1] == 2:
            return block
        return jnp.concatenate([block[:, :2], block[:, -2:]], axis=1)

    counts = piece_counts(local)
    pieces = len(counts)
    firsts = [sum(counts[:k]) for k in range(pieces)]
    bits = [1 << k for k in reversed(range(mems.bit_length() - 1))]
    coefficients = edges(jnp.stack([diffusivity, north_wind]))
    near, far = [], []
    for k in range(pieces):
        own = edges(ensemble[firsts[k] : firsts[k] + counts[k]])
        if k == 0:
            own = jnp.concatenate([coefficients, own], axis=0)
        near.append(lax.ppermute(own, "lat", near_pairs))
    for k in range(pieces):
        far.append(lax.ppermute(near[k], "lat", far_pairs))
    tables = observed_blocks[0], eastern_average_flags[0], observed_values[0], observed_error[0]
    top, low_bits = bits[0], bits[1:]

    def spread(a):
        held = [a]
        for bit in low_bits:
            held = held + [lax.ppermute(b, "mem", xor_pairs(mems, bit)) for b in held]
        return held

    masks = [0]
    for bit in low_bits:
        masks = masks + [m ^ bit for m in masks]
    masks = masks + [m ^ top for m in masks]
    near_half, far_half = [], []
    for k in range(pieces):
        band = pl.pallas_call(
            functools.partial(forecast_kernel, lats, firsts[k], counts[k], 2 if k == 0 else 0),
            out_shape=jax.ShapeDtypeStruct((counts[k], cell_count), F32),
            in_specs=[VMEM] * (7 + len(tables)),
            out_specs=VMEM,
            cost_estimate=pl.CostEstimate(flops=2000000, bytes_accessed=2000000, transcendentals=0),
            compiler_params=pltpu.CompilerParams(vmem_limit_bytes=8 << 20),
        )(ensemble, diffusivity, north_wind, near[k], far[k], near[0], far[0], *tables)
        far_half.append(lax.ppermute(band, "mem", xor_pairs(mems, top)))
        near_half.append(spread(band))

    def add_moments(stage, before, count):
        members = sum(a.shape[0] for a in stage)
        *after, stage_seen = pl.pallas_call(
            functools.partial(moment_kernel, len(before) > 0, count + members, longitudes),
            out_shape=[
                jax.ShapeDtypeStruct((observations, observations), F32),
                jax.ShapeDtypeStruct((observations, own_cells), F32),
                jax.ShapeDtypeStruct((1, observations), F32),
                jax.ShapeDtypeStruct((1, own_cells), F32),
                jax.ShapeDtypeStruct((members, observations), F32),
            ],
            in_specs=[SMEM] + [VMEM] * (1 + len(before) + len(stage)),
            out_specs=[VMEM] * 5,
            cost_estimate=pl.CostEstimate(flops=800000000, bytes_accessed=3000000, transcendentals=0),
            compiler_params=pltpu.CompilerParams(vmem_limit_bytes=16 << 20),
        )(*tables[:2], *before, *stage)
        return after, stage_seen

    stage = [near_half[k][j] for k in range(pieces) for j in range(mems // 2)]
    flat, order = stage, [(j, firsts[k]) for k in range(pieces) for j in range(mems // 2)]
    before, stage_seen = add_moments(stage, (), 0)
    seen = [stage_seen]
    for k in range(pieces):
        stage = spread(far_half[k])
        if k < pieces - 1:
            before, stage_seen = add_moments(stage, before, sum(a.shape[0] for a in flat))
            seen.append(stage_seen)
        flat = flat + stage
        order = order + [(j, firsts[k]) for j in range(mems // 2, mems)]
    near_parts = pieces * (mems // 2)
    near_order, far_order = order[:near_parts], [(j - mems // 2, row) for j, row in order[near_parts:]]
    to_member = jax.ShapeDtypeStruct((local, own_cells), F32)
    far_mems = mems - mems // 2
    part_of_product = [jax.ShapeDtypeStruct((observations, observations), BF16)] * 2
    part_of_cross = [jax.ShapeDtypeStruct((observations, own_cells), BF16)] * 2
    near_rows = local * (mems // 2)
    done = pl.pallas_call(
        functools.partial(
            gain_kernel, len(seen), len(stage), near_parts, near_order + far_order, longitudes
        ),
        out_shape=[to_member] * far_mems
        + [jax.ShapeDtypeStruct((near_rows, observations), F32)]
        + part_of_product * 3
        + part_of_cross,
        in_specs=[SMEM] + [VMEM] * (3 + len(before) + len(seen) + len(flat)),
        out_specs=[VMEM] * (far_mems + 9),
        scratch_shapes=[pltpu.VMEM((observations, observations), F32)],
        cost_estimate=pl.CostEstimate(flops=5000000000, bytes_accessed=4000000, transcendentals=0),
        compiler_params=pltpu.CompilerParams(vmem_limit_bytes=24 << 20),
        name="gain",
    )(*tables, *before, *seen, *flat)
    far_outs = done[:far_mems]
    near_outs = pl.pallas_call(
        functools.partial(finish_kernel, near_order),
        out_shape=[to_member] * (mems // 2),
        in_specs=[VMEM] * (9 + near_parts),
        out_specs=[VMEM] * (mems // 2),
        cost_estimate=pl.CostEstimate(flops=600000000, bytes_accessed=2000000, transcendentals=0),
        compiler_params=pltpu.CompilerParams(vmem_limit_bytes=16 << 20),
        name="finish",
    )(*done[far_mems:], *flat[:near_parts])
    outs = list(near_outs) + list(far_outs)
    came = {0: outs[0]}
    for mask in sorted(masks[1:], reverse=True):
        pairs = [(i, i ^ mask) for i in range(mems)]
        came[mask] = lax.ppermute(outs[masks.index(mask)], "mem", pairs)
    return pl.pallas_call(
        functools.partial(place_kernel, masks, longitudes),
        out_shape=jax.ShapeDtypeStruct((local, rows, longitudes), F32),
        in_specs=[VMEM] * mems,
        out_specs=pl.BlockSpec(memory_space=pl.ANY),
        scratch_shapes=[pltpu.VMEM((local, rows, longitudes), F32), pltpu.SemaphoreType.DMA((LOTS,))],
        cost_estimate=pl.CostEstimate(flops=100000, bytes_accessed=600000, transcendentals=0),
        compiler_params=pltpu.CompilerParams(vmem_limit_bytes=8 << 20),
        name="place",
    )(*[came[m] for m in masks])


def solution(mesh):
    return jax.shard_map(
        body,
        mesh=mesh,
        in_specs=(
            P("mem", "lat", None),
            P("lat", None),
            P("lat", None),
            P("lat", None, None),
            P("lat", None, None),
            P("lat", "mem", None),
            P("lat", "mem", None),
        ),
        out_specs=P("mem", "lat", None),
        check_vma=False,
    )
```

```python
import functools

import jax
import jax.numpy as jnp
from jax import lax
from jax.experimental import pallas as pl
from jax.experimental.pallas import tpu as pltpu
from jax.sharding import PartitionSpec as P


LOTS = 2
ADVECTION = 0.1
F32 = jnp.float32
BF16 = jnp.bfloat16
VMEM = pl.BlockSpec(memory_space=pltpu.VMEM)
SMEM = pl.BlockSpec(memory_space=pltpu.SMEM)


def xor_pairs(count, bit):
    return [(i, i ^ bit) for i in range(count)]


def piece_counts(local):
    unit = 8 if local % 8 == 0 else 1
    whole = local // unit
    first = (whole + 1) // 2
    return [n * unit for n in (first, whole - first) if n]


def step(rows, diffusivity, north_wind):
    out = []
    for r in range(1, len(rows) - 1):
        north, centre, south = rows[r - 1], rows[r], rows[r + 1]
        last = centre.shape[1] - 1
        eastern = pltpu.roll(centre, last, 1)
        western = pltpu.roll(centre, 1, 1)
        out.append(
            centre
            - ADVECTION * centre * (eastern - western)
            - north_wind[r - 1] * (south - north)
            + diffusivity[r - 1] * (eastern + western + north + south - 4.0 * centre)
        )
    return out


def forecast_kernel(lats, first, count, lead, own, dif, wind, near, far, coef_near, coef_far, *tables_and_out):
    out = tables_and_out[-1]
    place = lax.axis_index("lat")
    even = lax.rem(place, 2) == 0
    inner = (place > 0) & (place < lats - 1)
    rows, longitudes = own.shape[1], own.shape[2]
    edge = near.shape[1]

    def pick(a, b):
        return jnp.where(even, a, b)

    def members(ref, r):
        return ref[lead : lead + count, r, :]

    def beyond(x):
        return jnp.where(inner, x, 0.0)

    low = [pick(beyond(members(far, r)), members(near, r)) for r in (edge - 2, edge - 1)]
    high = [pick(members(near, r), beyond(members(far, r))) for r in (0, 1)]
    here = [own[first : first + count, r, :] for r in range(rows)]

    def coefficient(which, ref):
        before = pick(beyond(coef_far[which : which + 1, edge - 1, :]), coef_near[which : which + 1, edge - 1, :])
        after = pick(coef_near[which : which + 1, 0, :], beyond(coef_far[which : which + 1, 0, :]))
        return [before] + [ref[r : r + 1, :] for r in range(rows)] + [after]

    d, w = coefficient(0, dif), coefficient(1, wind)
    once = step(low + here + high, d, w)
    twice = step(once, d[1:-1], w[1:-1])
    for r in range(rows):
        out[:, r * longitudes : (r + 1) * longitudes] = twice[r]


def split(x):
    high = x.astype(BF16)
    return high, (x - high.astype(F32)).astype(BF16)


def dot3(a, b, width=256):
    rows = a[0].shape[0]
    mul = functools.partial(jnp.dot, preferred_element_type=F32)
    stacked = jnp.concatenate(a, axis=0)
    out = []
    for at in range(0, b[0].shape[1], width):
        both = mul(stacked, b[0][:, at : at + width])
        out.append(both[:rows] + (both[rows:] + mul(a[0], b[1][:, at : at + width])))
    return jnp.concatenate(out, axis=1)


def dot1(a, b, width=256):
    mul = functools.partial(jnp.dot, preferred_element_type=F32)
    return jnp.concatenate([mul(a, b[:, at : at + width]) for at in range(0, b.shape[1], width)], axis=1)


def observe(parts, longitudes, own_cells, blocks, flags):
    patch = lax.axis_index("mem")
    block_count = blocks.shape[1]
    width = flags.shape[1] // block_count
    row_blocks = longitudes // width
    flag = flags[pl.ds(patch, 1), :]
    lane = lax.broadcasted_iota(jnp.int32, (1, width), 1)
    columns = []
    for i in range(block_count):
        c = blocks[patch, i]
        row = lax.div(c, row_blocks)
        n = row * row_blocks + lax.rem(c - row * row_blocks + 1, row_blocks)
        averaged = flag[:, i * width : (i + 1) * width] == 1
        values = []
        for part in parts:
            direct = part[:, pl.ds(pl.multiple_of(c * width, width), width)]
            beyond = part[:, pl.ds(pl.multiple_of(n * width, width), width)]
            east = pltpu.roll(jnp.where(lane == 0, beyond, direct), width - 1, 1)
            values.append(jnp.where(averaged, 0.5 * (direct + east), direct))
        columns.append(jnp.concatenate(values, axis=0))
    return jnp.concatenate(columns, axis=1), own(parts, own_cells)


def own(parts, own_cells):
    at = pl.multiple_of(lax.axis_index("mem") * own_cells, own_cells)
    return jnp.concatenate([part[:, pl.ds(at, own_cells)] for part in parts], axis=0)


def doubled(x):
    high, low = split(x)
    return jnp.concatenate([high, high, low, low], axis=0)


def moments(seen, cells, before, count):
    if before is None:
        seen_mean = jnp.sum(seen, axis=0, keepdims=True) * (1.0 / count)
        cell_mean = jnp.sum(cells, axis=0, keepdims=True) * (1.0 / count)
        left = seen - seen_mean
        right, right_cells = left, cells - cell_mean
    else:
        left, right_cells = seen - before[0], cells - before[1]
        shift = jnp.sum(left, axis=0, keepdims=True) * (1.0 / count)
        cell_shift = jnp.sum(right_cells, axis=0, keepdims=True) * (1.0 / count)
        seen_mean, cell_mean = before[0] + shift, before[1] + cell_shift
        right, right_cells = left - shift, right_cells - cell_shift
    turned = jnp.concatenate(split(left), axis=0).T
    turned = jnp.concatenate([turned, turned], axis=1)
    return dot1(turned, doubled(right)), dot1(turned, doubled(right_cells)), seen_mean, cell_mean


def moment_kernel(has_before, count, longitudes, blocks, flags, *refs):
    refs = list(refs)
    outs = refs[-5:]
    before = refs[:4] if has_before else None
    parts = refs[4 if has_before else 0 : -5]
    seen, cells = observe(parts, longitudes, outs[1].shape[1], blocks, flags)
    means = None if before is None else (before[2][...], before[3][...])
    square, cross, seen_mean, cell_mean = moments(seen, cells, means, count)
    if before is not None:
        square, cross = square + before[0][...], cross + before[1][...]
    for out, value in zip(outs, (square, cross, seen_mean, cell_mean, seen)):
        out[...] = value


def square(x):
    half = x[0].shape[0] // 2
    first, second = slice(0, half), slice(half, 2 * half)

    def block(rows, columns):
        mul = functools.partial(jnp.dot, preferred_element_type=F32)
        (high, low), (high_right, low_right) = [p[rows] for p in x], [p[:, columns] for p in x]
        quarter = half // 2
        out = []
        for at in (0, quarter):
            h, l = high[at : at + quarter], low[at : at + quarter]
            both = mul(jnp.concatenate([h, l], axis=0), high_right)
            out.append(both[:quarter] + (both[quarter:] + mul(h, low_right)))
        return jnp.concatenate(out, axis=0)

    corner = block(first, second)
    above = jnp.concatenate([block(first, first), corner], axis=1)
    below = jnp.concatenate([corner.T, block(second, second)], axis=1)
    return jnp.concatenate([above, below], axis=0)


def gain_kernel(earlier, last, near_parts, order, longitudes, blocks, flags, values, errors, *refs):
    cov, left = refs[-1], refs[-11:-1]
    outs = refs[4 + earlier + len(order) : -11]
    before, first_seen, parts = refs[:4], refs[4 : 4 + earlier], refs[4 + earlier : 4 + earlier + len(order)]
    own_cells = outs[0].shape[1]
    total = sum(part.shape[0] for part in parts)
    last_seen, last_cells = observe(parts[-last:], longitudes, own_cells, blocks, flags)
    square_sum, cross, seen_mean, _ = moments(last_seen, last_cells, (before[2][...], before[3][...]), total)
    cov[...] = square_sum + before[0][...]
    tile = 128
    down = lax.broadcasted_iota(jnp.int32, (tile, tile), 0)
    across = lax.broadcasted_iota(jnp.int32, (tile, tile), 1)
    for at in range(0, cov.shape[0], tile):
        here = slice(at, at + tile)
        cov[here, here] += jnp.where(down == across, errors[:, here] * (total - 1.0), 0.0)
    covariance = cov[...]
    size = jnp.abs(covariance)
    root = lax.rsqrt(jnp.sum(size, axis=0, keepdims=True))
    root_down = lax.rsqrt(jnp.sum(size, axis=1, keepdims=True))
    cross = split((cross + before[1][...]) * root_down)
    seen = jnp.concatenate([ref[...] for ref in first_seen[1:]] + [last_seen], axis=0)
    start = weights(seen, seen_mean, values, root)
    b1 = (covariance * root_down) * root
    s1 = split(b1)
    b2 = 2.0 * b1 - square(s1)
    s2 = split(b2)
    b4 = 2.0 * b2 - square(s2)
    s4 = split(b4)
    for out, value in zip(left, (seen_mean, root) + s4 + s2 + s1 + cross):
        out[...] = value
    finish(start, s4, (s2, s1), cross, parts[near_parts:], order[near_parts:], outs)


def weights(seen, seen_mean, values, root):
    return ((values[...] - seen_mean) - 0.5 * (seen - seen_mean)) * root


def finish(start, s4, factors, cross, parts, order, outs):
    q = start + (start - dot1(start.astype(BF16), s4[0]))
    for _ in range(2):
        q = start + (q - dot3(split(q), s4))
    for factor in factors:
        q = 2.0 * q - dot3(split(q), factor)
    update = dot3(split(q), cross)
    at = 0
    for part, (j, row) in zip(parts, order):
        size = part.shape[0]
        outs[j][row : row + size, :] = own([part], outs[j].shape[1]) + update[at : at + size, :]
        at += size


def finish_kernel(order, seen, values, seen_mean, root, *refs):
    s4, s2, s1, cross = [(refs[i][...], refs[i + 1][...]) for i in (0, 2, 4, 6)]
    parts, outs = refs[8 : 8 + len(order)], refs[8 + len(order) :]
    start = weights(seen[...], seen_mean[...], values, root[...])
    finish(start, s4, (s2, s1), cross, parts, order, outs)


def place_kernel(masks, longitudes, *refs):
    sources, (out, laid, sems) = refs[:-3], refs[-3:]
    here = lax.axis_index("mem")
    lots = sems.shape[0]
    size = out.shape[0] // lots
    width = sources[0].shape[1]
    copies = []
    for lot in range(lots):
        members = slice(lot * size, (lot + 1) * size)
        found = [source[members, :] for source in sources]
        for patch in range(len(masks)):
            value = found[0]
            for m, candidate in zip(masks[1:], found[1:]):
                value = jnp.where((here ^ m) == patch, candidate, value)
            row, column = divmod(patch * width, longitudes)
            laid[members, row, column : column + width] = value
        copies.append(
            pltpu.make_async_copy(laid.at[pl.ds(lot * size, size)], out.at[pl.ds(lot * size, size)], sems.at[lot])
        )
        copies[-1].start()
    for copy in copies:
        copy.wait()


def body(
    ensemble,
    diffusivity,
    north_wind,
    observed_blocks,
    eastern_average_flags,
    observed_values,
    observed_error,
):
    local, rows, longitudes = ensemble.shape
    lats, mems = lax.axis_size("lat"), lax.axis_size("mem")
    observations = observed_values.shape[-1]
    cell_count = rows * longitudes
    own_cells = cell_count // mems
    near_pairs = xor_pairs(lats, 1)
    far_pairs = [(i, i + 2) for i in range(0, lats - 2, 2)] + [(i, i - 2) for i in range(3, lats, 2)]
    far_pairs += [(lats - 2, lats - 1), (1, 0)]

    def edges(block):
        if block.shape[1] == 2:
            return block
        return jnp.concatenate([block[:, :2], block[:, -2:]], axis=1)

    counts = piece_counts(local)
    pieces = len(counts)
    firsts = [sum(counts[:k]) for k in range(pieces)]
    bits = [1 << k for k in reversed(range(mems.bit_length() - 1))]
    coefficients = edges(jnp.stack([diffusivity, north_wind]))
    near, far = [], []
    for k in range(pieces):
        own = edges(ensemble[firsts[k] : firsts[k] + counts[k]])
        if k == 0:
            own = jnp.concatenate([coefficients, own], axis=0)
        near.append(lax.ppermute(own, "lat", near_pairs))
    for k in range(pieces):
        far.append(lax.ppermute(near[k], "lat", far_pairs))
    tables = observed_blocks[0], eastern_average_flags[0], observed_values[0], observed_error[0]
    top, low_bits = bits[0], bits[1:]

    def spread(a):
        held = [a]
        for bit in low_bits:
            held = held + [lax.ppermute(b, "mem", xor_pairs(mems, bit)) for b in held]
        return held

    masks = [0]
    for bit in low_bits:
        masks = masks + [m ^ bit for m in masks]
    masks = masks + [m ^ top for m in masks]
    near_half, far_half = [], []
    for k in range(pieces):
        band = pl.pallas_call(
            functools.partial(forecast_kernel, lats, firsts[k], counts[k], 2 if k == 0 else 0),
            out_shape=jax.ShapeDtypeStruct((counts[k], cell_count), F32),
            in_specs=[VMEM] * (7 + len(tables)),
            out_specs=VMEM,
            cost_estimate=pl.CostEstimate(flops=2000000, bytes_accessed=2000000, transcendentals=0),
            compiler_params=pltpu.CompilerParams(vmem_limit_bytes=8 << 20),
        )(ensemble, diffusivity, north_wind, near[k], far[k], near[0], far[0], *tables)
        far_half.append(lax.ppermute(band, "mem", xor_pairs(mems, top)))
        near_half.append(spread(band))

    def add_moments(stage, before, count):
        members = sum(a.shape[0] for a in stage)
        *after, stage_seen = pl.pallas_call(
            functools.partial(moment_kernel, len(before) > 0, count + members, longitudes),
            out_shape=[
                jax.ShapeDtypeStruct((observations, observations), F32),
                jax.ShapeDtypeStruct((observations, own_cells), F32),
                jax.ShapeDtypeStruct((1, observations), F32),
                jax.ShapeDtypeStruct((1, own_cells), F32),
                jax.ShapeDtypeStruct((members, observations), F32),
            ],
            in_specs=[SMEM] + [VMEM] * (1 + len(before) + len(stage)),
            out_specs=[VMEM] * 5,
            cost_estimate=pl.CostEstimate(flops=800000000, bytes_accessed=3000000, transcendentals=0),
            compiler_params=pltpu.CompilerParams(vmem_limit_bytes=16 << 20),
        )(*tables[:2], *before, *stage)
        return after, stage_seen

    stage = [near_half[k][j] for k in range(pieces) for j in range(mems // 2)]
    flat, order = stage, [(j, firsts[k]) for k in range(pieces) for j in range(mems // 2)]
    before, stage_seen = add_moments(stage, (), 0)
    seen = [stage_seen]
    for k in range(pieces):
        stage = spread(far_half[k])
        if k < pieces - 1:
            before, stage_seen = add_moments(stage, before, sum(a.shape[0] for a in flat))
            seen.append(stage_seen)
        flat = flat + stage
        order = order + [(j, firsts[k]) for j in range(mems // 2, mems)]
    near_parts = pieces * (mems // 2)
    near_order, far_order = order[:near_parts], [(j - mems // 2, row) for j, row in order[near_parts:]]
    to_member = jax.ShapeDtypeStruct((local, own_cells), F32)
    far_mems = mems - mems // 2
    part_of_product = [jax.ShapeDtypeStruct((observations, observations), BF16)] * 2
    part_of_cross = [jax.ShapeDtypeStruct((observations, own_cells), BF16)] * 2
    done = pl.pallas_call(
        functools.partial(
            gain_kernel, len(seen), len(stage), near_parts, near_order + far_order, longitudes
        ),
        out_shape=[to_member] * far_mems
        + [jax.ShapeDtypeStruct((1, observations), F32)] * 2
        + part_of_product * 3
        + part_of_cross,
        in_specs=[SMEM] + [VMEM] * (3 + len(before) + len(seen) + len(flat)),
        out_specs=[VMEM] * (far_mems + 10),
        scratch_shapes=[pltpu.VMEM((observations, observations), F32)],
        cost_estimate=pl.CostEstimate(flops=5000000000, bytes_accessed=4000000, transcendentals=0),
        compiler_params=pltpu.CompilerParams(vmem_limit_bytes=24 << 20),
        name="gain",
    )(*tables, *before, *seen, *flat)
    far_outs = done[:far_mems]
    near_outs = pl.pallas_call(
        functools.partial(finish_kernel, near_order),
        out_shape=[to_member] * (mems // 2),
        in_specs=[VMEM] * (12 + near_parts),
        out_specs=[VMEM] * (mems // 2),
        cost_estimate=pl.CostEstimate(flops=600000000, bytes_accessed=2000000, transcendentals=0),
        compiler_params=pltpu.CompilerParams(vmem_limit_bytes=16 << 20),
        name="finish",
    )(seen[0], observed_values[0], *done[far_mems:], *flat[:near_parts])
    outs = list(near_outs) + list(far_outs)
    came = {0: outs[0]}
    for mask in sorted(masks[1:], reverse=True):
        pairs = [(i, i ^ mask) for i in range(mems)]
        came[mask] = lax.ppermute(outs[masks.index(mask)], "mem", pairs)
    return pl.pallas_call(
        functools.partial(place_kernel, masks, longitudes),
        out_shape=jax.ShapeDtypeStruct((local, rows, longitudes), F32),
        in_specs=[VMEM] * mems,
        out_specs=pl.BlockSpec(memory_space=pl.ANY),
        scratch_shapes=[pltpu.VMEM((local, rows, longitudes), F32), pltpu.SemaphoreType.DMA((LOTS,))],
        cost_estimate=pl.CostEstimate(flops=100000, bytes_accessed=600000, transcendentals=0),
        compiler_params=pltpu.CompilerParams(vmem_limit_bytes=8 << 20),
        name="place",
    )(*[came[m] for m in masks])


def solution(mesh):
    return jax.shard_map(
        body,
        mesh=mesh,
        in_specs=(
            P("mem", "lat", None),
            P("lat", None),
            P("lat", None),
            P("lat", None, None),
            P("lat", None, None),
            P("lat", "mem", None),
            P("lat", "mem", None),
        ),
        out_specs=P("mem", "lat", None),
        check_vma=False,
    )
```
